256 devices in a mesh: ctx: 64 (over z, x, core), head: 4 (over y).
Axes of the slice: x: 4, y: 4, z: 8, core: 2. Of those that a mesh axis runs over, the one named last changes fastest.
Arguments:
- queries: float32 [16384, 4096], P('ctx', 'head'), may hold values from -48 to 48
- keys: float32 [16384, 4096], P('ctx', 'head'), may hold values from -48 to 48
- values: float32 [16384, 4096], P('ctx', 'head'), may hold values from -8 to 8
- query_map: float32 [32, 128, 128], P('head'), may hold values from -2 to 2
- key_map: float32 [32, 128, 128], P('head'), may hold values from -2 to 2
- out_weight: float32 [4096, 4096], P(None, ('ctx', 'head')), may hold values from -0.09375 to 0.09375
- residual: float32 [16384, 4096], P('ctx', 'head'), may hold values from -1.5 to 1.5
Outputs:
- layer_out: float32 [16384, 4096], P('ctx', 'head')
The draws below stay inside these ranges and needn't reach their ends.
All inputs are finite; a program needn't handle non-finite values.
Results may differ from the reference program's by a relative error of at most 0.0001.
Values sent between devices are 32-bit elements; how exact they have to be, the bound alone decides.
A program may use at most 192 MiB of HBM per device.

```python
import math
import jax
import jax.numpy as jnp
from jax import lax

D = 4096
H = 32
HD = 128
F = 128
TOKENS = 16384


def map_draw(key, salt):
    weights = jax.random.normal(jax.random.fold_in(key, salt), (H, HD, F), jnp.float32) * (2.0 / math.sqrt(HD))
    return jnp.clip(weights, -2.0, 2.0)


def drift_draw(key, salt):
    cycle_key, phase_key, level_key = jax.random.split(jax.random.fold_in(key, salt), 3)
    cycles = jax.random.uniform(cycle_key, (1, H, HD), jnp.float32, 0.5, 3.0)
    phase = jax.random.uniform(phase_key, (1, H, HD), jnp.float32, -math.pi, math.pi)
    levels = jax.random.uniform(level_key, (1, H, HD), jnp.float32, 0.5, 1.5)
    position = jnp.arange(TOKENS, dtype=jnp.float32)[:, None, None] / TOKENS
    return levels * jnp.sin(2.0 * math.pi * cycles * position + phase)


def input_draw(key, salt, drifting):
    base = jnp.clip(jax.random.normal(jax.random.fold_in(key, salt), (TOKENS, H, HD), jnp.float32), -6.0, 6.0)
    if drifting:
        base = base + drift_draw(key, salt + 200)
    return jnp.clip(base, -48.0, 48.0).reshape(TOKENS, D)


def draw_query_map(key, part):
    return map_draw(key, 11)


def draw_key_map(key, part):
    return map_draw(key, 12)


def draw_queries(key, part):
    return input_draw(key, 21, False)


def draw_keys(key, part):
    return input_draw(key, 22, True)


def draw_values(key, part):
    noise_key, offset_key = jax.random.split(jax.random.fold_in(key, 31))
    noise = jnp.clip(jax.random.normal(noise_key, (TOKENS, H, HD), jnp.float32), -4.0, 4.0)
    offset = jax.random.uniform(offset_key, (1, H, HD), jnp.float32, -1.0, 1.0)
    total = noise + offset + drift_draw(key, 33)
    return jnp.clip(total, -8.0, 8.0).reshape(TOKENS, D)


def steps_of(key, extent, cuts, least, top_value):
    def one(dim, parts):
        heights = jax.random.uniform(jax.random.fold_in(jax.random.fold_in(key, 6), dim), (parts,), jnp.float32, least / len(cuts), top_value / len(cuts))
        return jnp.repeat(jnp.exp(heights), extent[dim] // parts).reshape((-1,) + (1,) * (len(extent) - dim - 1))

    loudness = one(*cuts[0])
    for cut in cuts[1:]:
        loudness = loudness * one(*cut)
    return loudness


def bell_draw(rng, extent, scale, limit, cuts=(), kind=jnp.bfloat16):
    factor_of = steps_of(rng, extent, cuts, -0.22, 0.18) if cuts else 1.0
    entries = jax.random.normal(rng, extent, jnp.float32) * scale * factor_of
    return jnp.minimum(jnp.maximum(entries, -limit), limit).astype(kind)


def setup_inputs(seed: int = 0) -> dict:
    splits = jax.random.split(jax.random.key(seed), 8)
    queries = draw_queries(jax.random.fold_in(splits[7], 71), 0)
    keys = draw_keys(jax.random.fold_in(splits[7], 71), 0)
    values = draw_values(jax.random.fold_in(splits[7], 71), 0)
    query_map = draw_query_map(jax.random.fold_in(splits[7], 71), 0)
    key_map = draw_key_map(jax.random.fold_in(splits[7], 71), 0)
    out_weight = bell_draw(splits[5], (D, D), D ** -0.5, 0.09375, ((1, 256),), jnp.float32)
    residual = bell_draw(splits[6], (TOKENS, D), 0.25, 1.5, ((0, 64), (1, 4)), jnp.float32)
    return {"queries": queries, "keys": keys, "values": values, "query_map": query_map, "key_map": key_map, "out_weight": out_weight, "residual": residual}


HIGH = lax.Precision.HIGHEST


def feature_map(inputs, weights):
    scores = jnp.einsum("nhd,hdf->hnf", inputs, weights, precision=HIGH)
    return jnp.concatenate([jax.nn.softmax(scores, axis=-1), jax.nn.softmax(-scores, axis=-1)], axis=-1)


def reference(queries, keys, values, query_map, key_map, out_weight, residual):
    block = math.gcd(TOKENS, 512)
    count = TOKENS // block
    causal = jnp.tril(jnp.ones((block, block), jnp.float32))

    def split_rows(array):
        return array.reshape(count, block, H, HD)

    def advance(carry, pieces):
        state, norm = carry
        q_block, k_block, v_block = pieces
        query_feat = feature_map(q_block, query_map)
        key_feat = feature_map(k_block, key_map)
        value_heads = v_block.transpose(1, 0, 2)
        weights = jnp.einsum("hqf,hkf->hqk", query_feat, key_feat, precision=HIGH) * causal
        numer = jnp.einsum("hqk,hkd->hqd", weights, value_heads, precision=HIGH)
        numer = numer + jnp.einsum("hqf,hfd->hqd", query_feat, state, precision=HIGH)
        denom = jnp.sum(weights, axis=-1) + jnp.einsum("hqf,hf->hq", query_feat, norm, precision=HIGH)
        mixed = (numer / denom[..., None]).transpose(1, 0, 2).reshape(block, D)
        state = state + jnp.einsum("hkf,hkd->hfd", key_feat, value_heads, precision=HIGH)
        norm = norm + jnp.sum(key_feat, axis=1)
        return (state, norm), mixed

    start = (jnp.zeros((H, 2 * F, HD), jnp.float32), jnp.zeros((H, 2 * F), jnp.float32))
    _, mixed = lax.scan(advance, start, (split_rows(queries), split_rows(keys), split_rows(values)))
    mixed = mixed.reshape(TOKENS, D)
    return residual + jnp.dot(mixed, out_weight, precision=HIGH, preferred_element_type=jnp.float32)
```

```python
import jax
import jax.numpy as jnp
from jax import lax
from jax.experimental import pallas as pl
from jax.experimental.pallas import tpu as pltpu
from jax.sharding import PartitionSpec as P

MESH = pl.DeviceIdType.MESH
NX, NY, NZ = 4, 4, 8
ROWS, HEADS, HD, FEAT = 256, 8, 128, 256
WIDTH = HEADS * HD
HALF = 2048
KX = 1280
KZ = HALF - KX
SUBS = ((0, 72), (72, 64))
SROWS = 136
CHUNKS = 2
CR = ROWS // CHUNKS
F32, BF16 = jnp.float32, jnp.bfloat16

NN = (((1,), (0,)), ((), ()))
NT = (((1,), (1,)), ((), ()))


def split(a):
    high = a.astype(BF16)
    return high, (a - high.astype(F32)).astype(BF16)


def dot3(a, b, dims):
    (ah, al), (bh, bl) = a, b

    def one(p, q):
        return lax.dot_general(p, q, dims, preferred_element_type=F32)

    return one(ah, bh) + (one(ah, bl) + one(al, bh))


def features(inputs, weights):
    s = dot3(split(inputs), split(weights), NN)
    up = jnp.exp(s - jnp.max(s, axis=1, keepdims=True))
    down = jnp.exp(jnp.min(s, axis=1, keepdims=True) - s)
    up = up / jnp.sum(up, axis=1, keepdims=True)
    down = down / jnp.sum(down, axis=1, keepdims=True)
    return jnp.concatenate([up, down], axis=1)


def kernel(
    q_ref, k_ref, v_ref, qm_ref, km_ref, wt_ref, out_ref,
    qfh, qfl, kfh, kfl, nl, dl, st, rr, bk, pf, zp, zs,
    wb, wh, wl, ab, ah, al, co, cs, cr, fr,
    yg_s, yg_r, xa_s, xa_r, zx_s, zx_r, zz_s, zz_r, xz_s, xz_r,
    aa_s, aa_r, ch_s, ch_r, bb_s, bb_r, m_s, m_r, c_s, c_r, f_s, f_r,
):
    ctx, y = lax.axis_index("ctx"), lax.axis_index("head")
    core, r = lax.rem(ctx, 2), lax.rem(ctx, 8)
    x, z = lax.div(r, 2), lax.div(ctx, 8)
    row0 = ctx - r
    yp = lax.rem(y, 2)
    pair = y + 1 - 2 * yp
    far = 3 - y
    other = ctx + 1 - 2 * core
    pending = []

    def at(zz, xx):
        return ((zz * NX + xx) * 2 + core, y)

    def copy(src, dst, send, recv, device):
        return pltpu.make_async_remote_copy(
            src_ref=src, dst_ref=dst, send_sem=send, recv_sem=recv, device_id=device, device_id_type=MESH
        )

    def send(src, dst, ss, rs, device, when=None):
        c = copy(src, dst, ss, rs, device)
        if when is None:
            c.start()
        else:
            pl.when(when)(c.start)
        pending.append((when, c))

    def recv(dst, rs, when=None):
        c = copy(dst, dst, rs, rs, (ctx, y))
        if when is None:
            c.wait_recv()
        else:
            pl.when(when)(c.wait_recv)

    def member(zz):
        a = jnp.where(lax.rem(zz + 2, NZ) < 4, 0, 1)
        return jnp.logical_or(y == a, y == 3 - a)

    def slot(zz):
        return lax.rem(zz, 2) + jnp.where(lax.div(zz, 2) == y, 0, 2)

    barrier = pltpu.get_barrier_semaphore()
    greeted = [(ctx, lax.rem(y + i, NY)) for i in range(1, NY)]
    greeted += [(row0 + lax.rem(r + i, 8), y) for i in range(1, 8)]
    greeted += [at(lax.rem(z + 1, NZ), x), at(lax.rem(z + NZ - 1, NZ), x)]
    for device in greeted:
        pl.semaphore_signal(barrier, inc=1, device_id=device, device_id_type=MESH)
    pl.semaphore_wait(barrier, len(greeted))

    mine = member(z)
    my_slot = slot(z)
    first = jnp.where(lax.rem(z + 2, NZ) < 4, 0, 1)
    my_rows = pl.ds(pl.multiple_of(16 * y, 16), 16)
    for part in range(2):
        to = first if part == 0 else 3 - first
        there = lax.rem(z, 2) + jnp.where(lax.div(z, 2) == to, 0, 2)
        src = wt_ref.at[:, pl.ds(part * HALF, HALF)]
        send(src, wb.at[there, x, my_rows, :], yg_s.at[part], yg_r.at[y], (ctx, to), to != y)

        @pl.when(to == y)
        def _(there=there, part=part):
            wb[there, x, my_rows, :] = wt_ref[:, part * HALF : (part + 1) * HALF]

    def weights_y_done():
        for i in range(1, NY):
            yy = lax.rem(y + i, NY)
            recv(wb.at[my_slot, x, pl.ds(pl.multiple_of(16 * yy, 16), 16), :], yg_r.at[yy], mine)

    def weights_x_send():
        for i in range(1, NX):
            xx = lax.rem(x + i, NX)
            block = wb.at[my_slot, x, :, pl.ds(KZ, KX)]
            send(block, block, xa_s.at[i - 1], xa_r.at[x], at(z, xx), mine)

    def weights_x_done():
        for i in range(1, NX):
            xx = lax.rem(x + i, NX)
            recv(wb.at[my_slot, xx, :, pl.ds(KZ, KX)], xa_r.at[xx], mine)

    def ring(zz, d, n):
        return lax.rem(zz + (n if d == 0 else NZ - n) + NZ, NZ)

    def ring_x(d, s, i):
        xx = lax.rem(x + i, NX)
        source = ring(z, 1 - d, s)
        block = wb.at[slot(source), xx, :, pl.ds(KZ + d * (KX // 2), KX // 2)]
        have = member(source)
        if s > 0:
            recv(block, zx_r.at[d, s - 1, xx], have)
        if s < NZ - 1:
            send(block, block, zx_s.at[d, s, xx], zx_r.at[d, s, xx], at(ring(z, d, 1), x), have)

    def ring_z(d, s):
        source = ring(z, 1 - d, s)
        block = wb.at[slot(source), x, :, pl.ds(d * (KZ // 2), KZ // 2)]
        have = member(source)
        if s > 0:
            recv(block, zz_r.at[d, s - 1], have)
        if s < NZ - 1:
            send(block, block, zz_s.at[d, s], zz_r.at[d, s], at(ring(z, d, 1), x), have)
        for i in range(1, NX):
            xx = lax.rem(x + i, NX)
            send(block, block, xz_s.at[d, s, i - 1], xz_r.at[d, s, x], at(z, xx), have)

    def ring_z_done(d, s):
        source = ring(z, 1 - d, s)
        for i in range(1, NX):
            xx = lax.rem(x + i, NX)
            recv(wb.at[slot(source), xx, :, pl.ds(d * (KZ // 2), KZ // 2)], xz_r.at[d, s, xx], member(source))

    def weights_split():
        def one(i, carry):
            zi, xx = lax.div(i, NX), lax.rem(i, NX)
            high, low = split(wb[zi, xx])
            rows = pl.ds(pl.multiple_of(i * 64, 64), 64)
            wh[rows, :] = high
            wl[rows, :] = low
            return carry

        lax.fori_loop(0, 16, one, 0)

    def keys(h):
        cols = slice(h * HD, (h + 1) * HD)
        kf = features(k_ref[:, cols], km_ref[h])
        high, low = split(kf)
        kfh[h] = high
        kfl[h] = low
        st[h, 0:HD, :] = dot3(split(v_ref[:, cols].T), (high, low), NN)
        st[h, HD:SROWS, :] = jnp.broadcast_to(jnp.sum(kf, axis=0, keepdims=True), (SROWS - HD, FEAT))
        for n, (start, size) in enumerate(SUBS):
            rows = pl.ds(start, size)
            send(st.at[h, rows, :], rr.at[r, rows, :], aa_s.at[h, n], aa_r.at[r, n], (row0 + h, y), r != h)

        @pl.when(r == h)
        def _():
            rr[h] = st[h]

    def queries(h):
        cols = slice(h * HD, (h + 1) * HD)
        qf = split(features(q_ref[:, cols], qm_ref[h]))
        qfh[h], qfl[h] = qf
        w = dot3(qf, (kfh[h], kfl[h]), NT)
        causal = lax.broadcasted_iota(jnp.int32, (ROWS, ROWS), 0) >= lax.broadcasted_iota(jnp.int32, (ROWS, ROWS), 1)
        w = jnp.where(causal, w, 0.0)
        dl[h] = jnp.broadcast_to(jnp.sum(w, axis=1, keepdims=True), (ROWS, HD))
        nl[h] = dot3(split(w), split(v_ref[:, cols]), NN)

    def row_sums(n):
        start, size = SUBS[n]
        rows = pl.ds(start, size)
        for i in range(1, 8):
            j = lax.rem(r + i, 8)
            recv(rr.at[j, rows, :], aa_r.at[j, n])
        total = jnp.zeros((size, FEAT), F32)
        for i in range(8):
            bk[i, start : start + size, :] = total
            total = total + rr[i, start : start + size, :]
        zs[start : start + size, :] = total

    def chain(n):
        start, size = SUBS[n]
        rows = pl.ds(start, size)
        recv(zp.at[rows, :], ch_r.at[n], z > 0)

        @pl.when(z == 0)
        def _():
            zp[start : start + size, :] = jnp.zeros((size, FEAT), F32)

        @pl.when(z > 0)
        def _():
            zs[start : start + size, :] += zp[start : start + size, :]

        send(zs.at[rows, :], zp.at[rows, :], ch_s.at[n], ch_r.at[n], at(lax.rem(z + 1, NZ), x), z < NZ - 1)

    def send_back(n):
        start, size = SUBS[n]
        rows = pl.ds(start, size)
        before = zp[start : start + size, :]
        for i in range(8):
            bk[i, start : start + size, :] += before
            send(bk.at[i, rows, :], pf.at[r, rows, :], bb_s.at[i, n], bb_r.at[r, n], (row0 + i, y), r != i)

            @pl.when(r == i)
            def _(i=i):
                pf[i, start : start + size, :] = bk[i, start : start + size, :]

    def prefix_done():
        for n, (start, size) in enumerate(SUBS):
            for i in range(1, 8):
                j = lax.rem(r + i, 8)
                recv(pf.at[j, pl.ds(start, size), :], bb_r.at[j, n])

    def mix(c):
        rows = pl.ds(c * CR, CR)
        for h in range(HEADS):
            state = pf[h]
            qf = (qfh[h, c * CR : (c + 1) * CR, :], qfl[h, c * CR : (c + 1) * CR, :])
            far_sum = dot3(qf, split(state), NT)
            denom = dl[h, c * CR : (c + 1) * CR, :] + far_sum[:, HD : HD + 1]
            ab[yp, core, rows, h * HD : (h + 1) * HD] = (nl[h, c * CR : (c + 1) * CR, :] + far_sum[:, :HD]) / denom
        block = ab.at[yp, core, rows, :]
        send(block, block, m_s.at[c, 0], m_r.at[c, 0], (ctx, pair))
        send(block, block, m_s.at[c, 1], m_r.at[c, 1], (other, y))

    def relay(c):
        rows = pl.ds(c * CR, CR)
        block = ab.at[1 - yp, core, rows, :]
        recv(block, m_r.at[c, 0])
        send(block, block, m_s.at[c, 2], m_r.at[c, 2], (other, y))

    def project(c):
        rows = pl.ds(c * CR, CR)
        recv(ab.at[yp, 1 - core, rows, :], m_r.at[c, 1])
        recv(ab.at[1 - yp, 1 - core, rows, :], m_r.at[c, 2])
        for cc in range(2):
            for yy in range(2):
                high, low = split(ab[yy, cc, c * CR : (c + 1) * CR, :])
                ah[cc * CR : (cc + 1) * CR, yy * WIDTH : (yy + 1) * WIDTH] = high
                al[cc * CR : (cc + 1) * CR, yy * WIDTH : (yy + 1) * WIDTH] = low
        for base, dst in ((512, cs), (0, co)):

            def one(n, carry, base=base, dst=dst):
                wrows = pl.ds(pl.multiple_of(base + n * 256, 256), 256)
                cols = pl.ds(pl.multiple_of(n * 256, 256), 256)
                dst[c, :, cols] = dot3((ah[...], al[...]), (wh[wrows, :], wl[wrows, :]), NT)
                return carry

            lax.fori_loop(0, 2, one, 0)
            if base:
                send(cs.at[c], cr.at[c], c_s.at[c], c_r.at[c], (ctx, far))

    def gather(c):
        recv(cr.at[c], c_r.at[c])
        co[c] += cr[c]
        theirs = co.at[c, pl.ds(pl.multiple_of((1 - core) * CR, CR), CR), :]
        send(theirs, fr.at[c], f_s.at[c], f_r.at[c], (other, y))

    def finish(c):
        recv(fr.at[c], f_r.at[c])
        low_half = lax.broadcasted_iota(jnp.int32, (CR, 128), 1) < 64
        for cc in range(2):

            @pl.when(core == cc)
            def _(cc=cc):
                for m in range(4):
                    cols = slice(m * 128, (m + 1) * 128)
                    a, b = co[c, cc * CR : (cc + 1) * CR, cols], fr[c, :, cols]
                    if cc:
                        a, b = b, a
                    out_ref[c * CR : (c + 1) * CR, m * 256 : m * 256 + 128] = jnp.where(low_half, a, pltpu.roll(b, 64, 1))
                    out_ref[c * CR : (c + 1) * CR, m * 256 + 128 : (m + 1) * 256] = jnp.where(
                        low_half, pltpu.roll(a, 64, 1), b
                    )

    def ring_step(s):
        for i in range(NX):
            for d in range(2):
                ring_x(d, s, i)
        for d in range(2):
            ring_z(d, s)

    for h in range(HEADS):
        keys(h)
        if h == 3:
            weights_y_done()
            weights_x_send()
            for d in range(2):
                ring_z(d, 0)
    weights_x_done()
    for i in range(NX):
        for d in range(2):
            ring_x(d, 0, i)
    for h in range(HEADS):
        queries(h)
        if h == 4:
            for n in range(len(SUBS)):
                row_sums(n)
    ring_step(1)
    for n in range(len(SUBS)):
        chain(n)
    for n in range(len(SUBS)):
        send_back(n)
    for s in range(2, NZ):
        ring_step(s)
    prefix_done()
    for c in range(CHUNKS):
        mix(c)
    for s in range(NZ):
        for d in range(2):
            ring_z_done(d, s)
    weights_split()
    relay(0)
    for c in range(CHUNKS):
        project(c)
        if c + 1 < CHUNKS:
            relay(c + 1)
        if c > 0:
            gather(c - 1)
    gather(CHUNKS - 1)
    for c in range(CHUNKS):
        finish(c)
    for when, c in pending:
        if when is None:
            c.wait_send()
        else:
            pl.when(when)(c.wait_send)


def attend(q, k, v, qm, km, wt):
    dma = pltpu.SemaphoreType.DMA
    subs = len(SUBS)
    vmem = pltpu.VMEM
    scratch = [
        vmem((HEADS, ROWS, FEAT), BF16), vmem((HEADS, ROWS, FEAT), BF16),
        vmem((HEADS, ROWS, FEAT), BF16), vmem((HEADS, ROWS, FEAT), BF16),
        vmem((HEADS, ROWS, HD), F32), vmem((HEADS, ROWS, HD), F32),
        vmem((HEADS, SROWS, FEAT), F32), vmem((HEADS, SROWS, FEAT), F32),
        vmem((HEADS, SROWS, FEAT), F32), vmem((HEADS, SROWS, FEAT), F32),
        vmem((SROWS, FEAT), F32), vmem((SROWS, FEAT), F32),
        vmem((4, NX, 64, HALF), F32), vmem((1024, HALF), BF16), vmem((1024, HALF), BF16),
        vmem((2, 2, ROWS, WIDTH), F32), vmem((2 * CR, HALF), BF16), vmem((2 * CR, HALF), BF16),
        vmem((CHUNKS, 2 * CR, 512), F32), vmem((CHUNKS, 2 * CR, 512), F32),
        vmem((CHUNKS, 2 * CR, 512), F32), vmem((CHUNKS, CR, 512), F32),
        dma((2,)), dma((NY,)), dma((3,)), dma((NX,)),
        dma((2, NZ - 1, NX)), dma((2, NZ - 1, NX)), dma((2, NZ - 1)), dma((2, NZ - 1)),
        dma((2, NZ, 3)), dma((2, NZ, NX)),
        dma((8, subs)), dma((8, subs)), dma((subs,)), dma((subs,)), dma((8, subs)), dma((8, subs)),
        dma((CHUNKS, 3)), dma((CHUNKS, 3)), dma((CHUNKS,)), dma((CHUNKS,)), dma((CHUNKS,)), dma((CHUNKS,)),
    ]
    return pl.pallas_call(
        kernel,
        out_shape=jax.ShapeDtypeStruct((ROWS, WIDTH), F32),
        in_specs=[pl.BlockSpec(memory_space=vmem)] * 6,
        out_specs=pl.BlockSpec(memory_space=vmem),
        scratch_shapes=scratch,
        compiler_params=pltpu.CompilerParams(
            collective_id=0, has_side_effects=True, vmem_limit_bytes=60 * 1024 * 1024
        ),
    )(q, k, v, qm, km, wt)


def body(queries, keys, values, query_map, key_map, out_weight, residual):
    return residual + attend(queries, keys, values, query_map, key_map, out_weight.T)


def solution(mesh):
    placed = (
        P("ctx", "head"),
        P("ctx", "head"),
        P("ctx", "head"),
        P("head", None, None),
        P("head", None, None),
        P(None, ("ctx", "head")),
        P("ctx", "head"),
    )
    return jax.shard_map(body, mesh=mesh, in_specs=placed, out_specs=P("ctx", "head"), check_vma=False)
```

```python
import jax
import jax.numpy as jnp
from jax import lax
from jax.experimental import pallas as pl
from jax.experimental.pallas import tpu as pltpu
from jax.sharding import PartitionSpec as P

MESH = pl.DeviceIdType.MESH
NX, NY, NZ = 4, 4, 8
ROWS, HEADS, HD, FEAT = 256, 8, 128, 256
WIDTH = HEADS * HD
HALF = 2048
KP = 1024
KZ = 384
KX = KP - KZ
ZHALF = ((0, 256), (256, 128))
SUBS = ((0, 72), (72, 64))
SROWS = 136
CHUNKS = 2
CR = ROWS // CHUNKS
F32, BF16 = jnp.float32, jnp.bfloat16

NN = (((1,), (0,)), ((), ()))
NT = (((1,), (1,)), ((), ()))


def split(a):
    high = a.astype(BF16)
    return high, (a - high.astype(F32)).astype(BF16)


def dot3(a, b, dims):
    (ah, al), (bh, bl) = a, b

    def one(p, q):
        return lax.dot_general(p, q, dims, preferred_element_type=F32)

    return one(ah, bh) + (one(ah, bl) + one(al, bh))


def features(inputs, weights):
    s = dot3(split(inputs), split(weights), NN)
    up = jnp.exp(s - jnp.max(s, axis=1, keepdims=True))
    down = jnp.exp(jnp.min(s, axis=1, keepdims=True) - s)
    up = up / jnp.sum(up, axis=1, keepdims=True)
    down = down / jnp.sum(down, axis=1, keepdims=True)
    return jnp.concatenate([up, down], axis=1)


def kernel(
    q_ref, k_ref, v_ref, qm_ref, km_ref, wt_ref, out_ref,
    qfh, qfl, kfh, kfl, nl, dl, st, rr, bk, pf, zp, zs,
    wb, wh, wl, ab, ah, al, co, cs, cr, fr,
    yg_s, yg_r, xa_s, xa_r, zx_s, zx_r, zz_s, zz_r, xz_s, xz_r,
    aa_s, aa_r, ch_s, ch_r, bb_s, bb_r, m_s, m_r, c_s, c_r, f_s, f_r,
):
    ctx, y = lax.axis_index("ctx"), lax.axis_index("head")
    core, r = lax.rem(ctx, 2), lax.rem(ctx, 8)
    x, z = lax.div(r, 2), lax.div(ctx, 8)
    row0 = ctx - r
    yp = lax.rem(y, 2)
    pair = y + 1 - 2 * yp
    far = 3 - y
    other = ctx + 1 - 2 * core
    pending = []

    def at(zz, xx):
        return ((zz * NX + xx) * 2 + core, y)

    def copy(src, dst, send, recv, device):
        return pltpu.make_async_remote_copy(
            src_ref=src, dst_ref=dst, send_sem=send, recv_sem=recv, device_id=device, device_id_type=MESH
        )

    def send(src, dst, ss, rs, device, when=None):
        c = copy(src, dst, ss, rs, device)
        if when is None:
            c.start()
        else:
            pl.when(when)(c.start)
        pending.append((when, c))

    def recv(dst, rs, when=None):
        c = copy(dst, dst, rs, rs, (ctx, y))
        if when is None:
            c.wait_recv()
        else:
            pl.when(when)(c.wait_recv)

    def member(zz):
        a = jnp.where(lax.rem(zz + 2, NZ) < 4, 0, 1)
        return jnp.logical_or(y == a, y == 3 - a)

    def slot(zz):
        return lax.rem(zz, 2) + jnp.where(lax.div(zz, 2) == y, 0, 2)

    def twin(zz):
        return zz + 2 - 4 * lax.rem(lax.div(zz, 2), 2)

    barrier = pltpu.get_barrier_semaphore()
    greeted = [(ctx, lax.rem(y + i, NY)) for i in range(1, NY)]
    greeted += [(row0 + lax.rem(r + i, 8), y) for i in range(1, 8)]
    greeted += [at(lax.rem(z + 1, NZ), x), at(lax.rem(z + NZ - 1, NZ), x)]
    greeted += [(at(twin(z), x)[0], lax.rem(y + i, NY)) for i in range(NY)]
    for device in greeted:
        pl.semaphore_signal(barrier, inc=1, device_id=device, device_id_type=MESH)
    pl.semaphore_wait(barrier, len(greeted))

    first = jnp.where(lax.rem(z + 2, NZ) < 4, 0, 1)
    my_rows = pl.ds(pl.multiple_of(16 * y, 16), 16)
    for part in range(2):
        to = first if part == 0 else 3 - first
        there = lax.rem(z, 2) + jnp.where(lax.div(z, 2) == to, 0, 2)
        low = slice(part * HALF, part * HALF + KP)
        dst = wb.at[there, x, my_rows, pl.ds(KP, KP)]
        send(wt_ref.at[:, pl.ds(part * HALF + KP, KP)], dst, yg_s.at[part, 1], yg_r.at[y], (at(twin(z), x)[0], to))
        dst = wb.at[there, x, my_rows, pl.ds(0, KP)]
        send(wt_ref.at[:, pl.ds(part * HALF, KP)], dst, yg_s.at[part, 0], yg_r.at[y], (ctx, to), to != y)

        @pl.when(to == y)
        def _(there=there, low=low):
            wb[there, x, my_rows, 0:KP] = wt_ref[:, low]

    def block_of(zz, xx, start, size):
        has = member(zz)
        at_slot = slot(jnp.where(has, zz, twin(zz)))
        cols = pl.ds(pl.multiple_of(jnp.where(has, start, KP + start), 128), size)
        return wb.at[at_slot, xx, :, cols]

    def weights_y_done():
        has = member(z)
        at_slot = slot(jnp.where(has, z, twin(z)))
        cols = pl.ds(pl.multiple_of(jnp.where(has, 0, KP), 128), KP)
        for i in range(NY):
            yy = lax.rem(y + i, NY)
            rows = pl.ds(pl.multiple_of(16 * yy, 16), 16)
            recv(wb.at[at_slot, x, rows, cols], yg_r.at[yy], jnp.logical_not(has) if i == 0 else None)

    def weights_x_send():
        for i in range(1, NX):
            xx = lax.rem(x + i, NX)
            block = block_of(z, x, KZ, KX)
            send(block, block, xa_s.at[i - 1], xa_r.at[x], at(z, xx))

    def weights_x_done(i):
        xx = lax.rem(x + i, NX)
        recv(block_of(z, xx, KZ, KX), xa_r.at[xx])

    def ring(zz, d, n):
        return lax.rem(zz + (n if d == 0 else NZ - n), NZ)

    def ring_x(d, s, i):
        xx = lax.rem(x + i, NX)
        block = block_of(ring(z, 1 - d, s), xx, KZ, KX)
        last = i // 2 == d
        if s > 0 and (s < 4 or last):
            recv(block, zx_r.at[d, s - 1, xx])
        if s < 3 or (s == 3 and last):
            send(block, block, zx_s.at[d, s, xx], zx_r.at[d, s, xx], at(ring(z, d, 1), x))

    def ring_z(d, s):
        source = ring(z, 1 - d, s)
        start, size = ZHALF[d] if s == 4 else (0, KZ)
        block = block_of(source, x, start, size)
        if s > 0:
            recv(block, zz_r.at[d, s - 1])
        if s < 4:
            start, size = ZHALF[d] if s == 3 else (0, KZ)
            part = block_of(source, x, start, size)
            send(part, part, zz_s.at[d, s], zz_r.at[d, s], at(ring(z, d, 1), x))
        if s > 0 or d == 0:
            for i in range(1, NX):
                xx = lax.rem(x + i, NX)
                send(block, block, xz_s.at[d, s, i - 1], xz_r.at[d, s, x], at(z, xx))

    def ring_z_done(d, s):
        source = ring(z, 1 - d, s)
        start, size = ZHALF[d] if s == 4 else (0, KZ)
        if s > 0 or d == 0:
            for i in range(1, NX):
                xx = lax.rem(x + i, NX)
                recv(block_of(source, xx, start, size), xz_r.at[d, s, xx])

    def weights_split():
        def one(i, carry):
            zi, xx = lax.div(i, NX), lax.rem(i, NX)
            high, low = split(wb[zi, xx])
            rows = pl.ds(pl.multiple_of(i * 64, 64), 64)
            wh[rows, :] = high
            wl[rows, :] = low
            return carry

        lax.fori_loop(0, 16, one, 0)

    def keys(h):
        cols = slice(h * HD, (h + 1) * HD)
        kf = features(k_ref[:, cols], km_ref[h])
        high, low = split(kf)
        kfh[h] = high
        kfl[h] = low
        st[h, 0:HD, :] = dot3(split(v_ref[:, cols].T), (high, low), NN)
        st[h, HD:SROWS, :] = jnp.broadcast_to(jnp.sum(kf, axis=0, keepdims=True), (SROWS - HD, FEAT))
        for n, (start, size) in enumerate(SUBS):
            rows = pl.ds(start, size)
            send(st.at[h, rows, :], rr.at[r, rows, :], aa_s.at[h, n], aa_r.at[r, n], (row0 + h, y), r != h)

        @pl.when(r == h)
        def _():
            rr[h] = st[h]

    def queries(h):
        cols = slice(h * HD, (h + 1) * HD)
        qf = split(features(q_ref[:, cols], qm_ref[h]))
        qfh[h], qfl[h] = qf
        w = dot3(qf, (kfh[h], kfl[h]), NT)
        causal = lax.broadcasted_iota(jnp.int32, (ROWS, ROWS), 0) >= lax.broadcasted_iota(jnp.int32, (ROWS, ROWS), 1)
        w = jnp.where(causal, w, 0.0)
        dl[h] = jnp.broadcast_to(jnp.sum(w, axis=1, keepdims=True), (ROWS, HD))
        nl[h] = dot3(split(w), split(v_ref[:, cols]), NN)

    def row_sums(n):
        start, size = SUBS[n]
        rows = pl.ds(start, size)
        for i in range(1, 8):
            j = lax.rem(r + i, 8)
            recv(rr.at[j, rows, :], aa_r.at[j, n])
        total = jnp.zeros((size, FEAT), F32)
        for i in range(8):
            bk[i, start : start + size, :] = total
            total = total + rr[i, start : start + size, :]
        zs[start : start + size, :] = total

    def chain(n):
        start, size = SUBS[n]
        rows = pl.ds(start, size)
        recv(zp.at[rows, :], ch_r.at[n], z > 0)

        @pl.when(z == 0)
        def _():
            zp[start : start + size, :] = jnp.zeros((size, FEAT), F32)

        @pl.when(z > 0)
        def _():
            zs[start : start + size, :] += zp[start : start + size, :]

        send(zs.at[rows, :], zp.at[rows, :], ch_s.at[n], ch_r.at[n], at(lax.rem(z + 1, NZ), x), z < NZ - 1)

    def send_back(n):
        start, size = SUBS[n]
        rows = pl.ds(start, size)
        before = zp[start : start + size, :]
        for i in range(8):
            bk[i, start : start + size, :] += before
            send(bk.at[i, rows, :], pf.at[r, rows, :], bb_s.at[i, n], bb_r.at[r, n], (row0 + i, y), r != i)

            @pl.when(r == i)
            def _(i=i):
                pf[i, start : start + size, :] = bk[i, start : start + size, :]

    def prefix_done():
        for n, (start, size) in enumerate(SUBS):
            for i in range(1, 8):
                j = lax.rem(r + i, 8)
                recv(pf.at[j, pl.ds(start, size), :], bb_r.at[j, n])

    def mix(c):
        rows = pl.ds(c * CR, CR)
        for h in range(HEADS):
            state = pf[h]
            qf = (qfh[h, c * CR : (c + 1) * CR, :], qfl[h, c * CR : (c + 1) * CR, :])
            far_sum = dot3(qf, split(state), NT)
            denom = dl[h, c * CR : (c + 1) * CR, :] + far_sum[:, HD : HD + 1]
            ab[yp, core, rows, h * HD : (h + 1) * HD] = (nl[h, c * CR : (c + 1) * CR, :] + far_sum[:, :HD]) / denom
        block = ab.at[yp, core, rows, :]
        send(block, block, m_s.at[c, 0], m_r.at[c, 0], (ctx, pair))
        send(block, block, m_s.at[c, 1], m_r.at[c, 1], (other, y))

    def relay(c):
        rows = pl.ds(c * CR, CR)
        block = ab.at[1 - yp, core, rows, :]
        recv(block, m_r.at[c, 0])
        send(block, block, m_s.at[c, 2], m_r.at[c, 2], (other, y))

    def project(c):
        rows = pl.ds(c * CR, CR)
        recv(ab.at[yp, 1 - core, rows, :], m_r.at[c, 1])
        recv(ab.at[1 - yp, 1 - core, rows, :], m_r.at[c, 2])
        for cc in range(2):
            for yy in range(2):
                high, low = split(ab[yy, cc, c * CR : (c + 1) * CR, :])
                ah[cc * CR : (cc + 1) * CR, yy * WIDTH : (yy + 1) * WIDTH] = high
                al[cc * CR : (cc + 1) * CR, yy * WIDTH : (yy + 1) * WIDTH] = low
        for base, dst in ((512, cs), (0, co)):

            def one(n, carry, base=base, dst=dst):
                wrows = pl.ds(pl.multiple_of(base + n * 256, 256), 256)
                cols = pl.ds(pl.multiple_of(n * 256, 256), 256)
                dst[c, :, cols] = dot3((ah[...], al[...]), (wh[wrows, :], wl[wrows, :]), NT)
                return carry

            lax.fori_loop(0, 2, one, 0)
            if base:
                send(cs.at[c], cr.at[c], c_s.at[c], c_r.at[c], (ctx, far))

    def gather(c):
        recv(cr.at[c], c_r.at[c])
        co[c] += cr[c]
        theirs = co.at[c, pl.ds(pl.multiple_of((1 - core) * CR, CR), CR), :]
        send(theirs, fr.at[c], f_s.at[c], f_r.at[c], (other, y))

    def finish(c):
        recv(fr.at[c], f_r.at[c])
        low_half = lax.broadcasted_iota(jnp.int32, (CR, 128), 1) < 64
        for cc in range(2):

            @pl.when(core == cc)
            def _(cc=cc):
                for m in range(4):
                    cols = slice(m * 128, (m + 1) * 128)
                    a, b = co[c, cc * CR : (cc + 1) * CR, cols], fr[c, :, cols]
                    if cc:
                        a, b = b, a
                    out_ref[c * CR : (c + 1) * CR, m * 256 : m * 256 + 128] = jnp.where(low_half, a, pltpu.roll(b, 64, 1))
                    out_ref[c * CR : (c + 1) * CR, m * 256 + 128 : (m + 1) * 256] = jnp.where(
                        low_half, pltpu.roll(a, 64, 1), b
                    )

    def ring_step(s):
        for i in range(NX):
            for d in range(2):
                ring_x(d, s, i)
            if i == 0:
                for d in range(2):
                    ring_z(d, s)

    for h in range(HEADS):
        keys(h)
        if h == 1:
            weights_y_done()
            weights_x_send()
            for d in range(2):
                ring_x(d, 0, 0)
                ring_z(d, 0)
        if h == 4:
            for i in range(1, NX):
                weights_x_done(i)
                for d in range(2):
                    ring_x(d, 0, i)
    for h in range(HEADS):
        queries(h)
        if h == 1:
            ring_step(1)
        if h == 4:
            for n in range(len(SUBS)):
                row_sums(n)
    for n in range(len(SUBS)):
        chain(n)
    ring_step(2)
    for n in range(len(SUBS)):
        send_back(n)
    ring_step(3)
    ring_step(4)
    prefix_done()
    for c in range(CHUNKS):
        mix(c)
    for s in range(5):
        for d in range(2):
            ring_z_done(d, s)
    weights_split()
    relay(0)
    for c in range(CHUNKS):
        project(c)
        if c + 1 < CHUNKS:
            relay(c + 1)
        if c > 0:
            gather(c - 1)
    gather(CHUNKS - 1)
    for c in range(CHUNKS):
        finish(c)
    for when, c in pending:
        if when is None:
            c.wait_send()
        else:
            pl.when(when)(c.wait_send)


def attend(q, k, v, qm, km, wt):
    dma = pltpu.SemaphoreType.DMA
    subs = len(SUBS)
    vmem = pltpu.VMEM
    scratch = [
        vmem((HEADS, ROWS, FEAT), BF16), vmem((HEADS, ROWS, FEAT), BF16),
        vmem((HEADS, ROWS, FEAT), BF16), vmem((HEADS, ROWS, FEAT), BF16),
        vmem((HEADS, ROWS, HD), F32), vmem((HEADS, ROWS, HD), F32),
        vmem((HEADS, SROWS, FEAT), F32), vmem((HEADS, SROWS, FEAT), F32),
        vmem((HEADS, SROWS, FEAT), F32), vmem((HEADS, SROWS, FEAT), F32),
        vmem((SROWS, FEAT), F32), vmem((SROWS, FEAT), F32),
        vmem((4, NX, 64, HALF), F32), vmem((1024, HALF), BF16), vmem((1024, HALF), BF16),
        vmem((2, 2, ROWS, WIDTH), F32), vmem((2 * CR, HALF), BF16), vmem((2 * CR, HALF), BF16),
        vmem((CHUNKS, 2 * CR, 512), F32), vmem((CHUNKS, 2 * CR, 512), F32),
        vmem((CHUNKS, 2 * CR, 512), F32), vmem((CHUNKS, CR, 512), F32),
        dma((2, 2)), dma((NY,)), dma((3,)), dma((NX,)),
        dma((2, 4, NX)), dma((2, 4, NX)), dma((2, 4)), dma((2, 4)),
        dma((2, 5, 3)), dma((2, 5, NX)),
        dma((8, subs)), dma((8, subs)), dma((subs,)), dma((subs,)), dma((8, subs)), dma((8, subs)),
        dma((CHUNKS, 3)), dma((CHUNKS, 3)), dma((CHUNKS,)), dma((CHUNKS,)), dma((CHUNKS,)), dma((CHUNKS,)),
    ]
    return pl.pallas_call(
        kernel,
        out_shape=jax.ShapeDtypeStruct((ROWS, WIDTH), F32),
        in_specs=[pl.BlockSpec(memory_space=vmem)] * 6,
        out_specs=pl.BlockSpec(memory_space=vmem),
        scratch_shapes=scratch,
        compiler_params=pltpu.CompilerParams(
            collective_id=0, has_side_effects=True, vmem_limit_bytes=60 * 1024 * 1024
        ),
    )(q, k, v, qm, km, wt)


def body(queries, keys, values, query_map, key_map, out_weight, residual):
    return residual + attend(queries, keys, values, query_map, key_map, out_weight.T)


def solution(mesh):
    placed = (
        P("ctx", "head"),
        P("ctx", "head"),
        P("ctx", "head"),
        P("head", None, None),
        P("head", None, None),
        P(None, ("ctx", "head")),
        P("ctx", "head"),
    )
    return jax.shard_map(body, mesh=mesh, in_specs=placed, out_specs=P("ctx", "head"), check_vma=False)
```

```python
import jax
import jax.numpy as jnp
from jax import lax
from jax.experimental import pallas as pl
from jax.experimental.pallas import tpu as pltpu
from jax.sharding import PartitionSpec as P

MESH = pl.DeviceIdType.MESH
NX, NY, NZ = 4, 4, 8
ROWS, HEADS, HD, FEAT = 256, 8, 128, 256
WIDTH = HEADS * HD
HALF = 2048
KP = 1024
KZ = 512
KX = KP - KZ
ZHALF = ((0, 256), (256, 256))
PIECE = 16
SROWS = 136
CHUNKS = 4
CR = ROWS // CHUNKS
F32, BF16 = jnp.float32, jnp.bfloat16

NN = (((1,), (0,)), ((), ()))
NT = (((1,), (1,)), ((), ()))


def split(a):
    high = a.astype(BF16)
    return high, (a - high.astype(F32)).astype(BF16)


def dot3(a, b, dims):
    (ah, al), (bh, bl) = a, b

    def one(p, q):
        return lax.dot_general(p, q, dims, preferred_element_type=F32)

    return one(ah, bh) + (one(ah, bl) + one(al, bh))


def features(inputs, weights):
    s = dot3(split(inputs), split(weights), NN)
    up = jnp.exp(s - jnp.max(s, axis=1, keepdims=True))
    down = jnp.exp(jnp.min(s, axis=1, keepdims=True) - s)
    up = up / jnp.sum(up, axis=1, keepdims=True)
    down = down / jnp.sum(down, axis=1, keepdims=True)
    return jnp.concatenate([up, down], axis=1)


def kernel(
    q_ref, k_ref, v_ref, qm_ref, km_ref, wt_ref, out_ref,
    qfh, qfl, kfh, kfl, nl, dl, st, sp, su, rr, bk, pc, sd, pf, zt, zr, zb, zp,
    wb, wh, wl, ab, ah, al, co, cs, cr, fr,
    yg_s, yg_r, xa_s, xa_r, zx_s, zx_r, zz_s, zz_r, xz_s, xz_r,
    dd_s, dd_r, aa_s, aa_r, z1_s, z1_r, z2_s, z2_r, bb_s, bb_r, ee_s, ee_r, m_s, m_r, c_s, c_r, f_s, f_r,
):
    ctx, y = lax.axis_index("ctx"), lax.axis_index("head")
    core, r = lax.rem(ctx, 2), lax.rem(ctx, 8)
    x, z = lax.div(r, 2), lax.div(ctx, 8)
    yp = lax.rem(y, 2)
    pair = y + 1 - 2 * yp
    far = 3 - y
    other = ctx + 1 - 2 * core
    pending = []

    def at(zz, xx):
        return ((zz * NX + xx) * 2 + core, y)

    def copy(src, dst, send, recv, device):
        return pltpu.make_async_remote_copy(
            src_ref=src, dst_ref=dst, send_sem=send, recv_sem=recv, device_id=device, device_id_type=MESH
        )

    def send(src, dst, ss, rs, device, when=None):
        c = copy(src, dst, ss, rs, device)
        if when is None:
            c.start()
        else:
            pl.when(when)(c.start)
        pending.append((when, c))

    def recv(dst, rs, when=None):
        c = copy(dst, dst, rs, rs, (ctx, y))
        if when is None:
            c.wait_recv()
        else:
            pl.when(when)(c.wait_recv)

    def member(zz):
        a = jnp.where(lax.rem(zz + 2, NZ) < 4, 0, 1)
        return jnp.logical_or(y == a, y == 3 - a)

    def slot(zz):
        return lax.rem(zz, 2) + jnp.where(lax.div(zz, 2) == y, 0, 2)

    def twin(zz):
        return zz + 2 - 4 * lax.rem(lax.div(zz, 2), 2)

    barrier = pltpu.get_barrier_semaphore()
    greeted = [(ctx, lax.rem(y + i, NY)) for i in range(1, NY)]
    greeted += [at(z, lax.rem(x + i, NX)) for i in range(1, NX)] + [(other, y)]
    greeted += [at(lax.rem(z + i, NZ), x) for i in range(1, NZ)]
    greeted += [(at(twin(z), x)[0], lax.rem(y + i, NY)) for i in range(1, NY)]
    for device in greeted:
        pl.semaphore_signal(barrier, inc=1, device_id=device, device_id_type=MESH)
    pl.semaphore_wait(barrier, len(greeted))

    first = jnp.where(lax.rem(z + 2, NZ) < 4, 0, 1)
    my_rows = pl.ds(pl.multiple_of(16 * y, 16), 16)
    for part in range(2):
        to = first if part == 0 else 3 - first
        there = lax.rem(z, 2) + jnp.where(lax.div(z, 2) == to, 0, 2)
        low = slice(part * HALF, part * HALF + KP)
        dst = wb.at[there, x, my_rows, pl.ds(KP, KP)]
        send(wt_ref.at[:, pl.ds(part * HALF + KP, KP)], dst, yg_s.at[part, 1], yg_r.at[y], (at(twin(z), x)[0], to))
        dst = wb.at[there, x, my_rows, pl.ds(0, KP)]
        send(wt_ref.at[:, pl.ds(part * HALF, KP)], dst, yg_s.at[part, 0], yg_r.at[y], (ctx, to), to != y)

        @pl.when(to == y)
        def _(there=there, low=low):
            wb[there, x, my_rows, 0:KP] = wt_ref[:, low]

    def block_of(zz, xx, start, size):
        has = member(zz)
        at_slot = slot(jnp.where(has, zz, twin(zz)))
        cols = pl.ds(pl.multiple_of(jnp.where(has, start, KP + start), 128), size)
        return wb.at[at_slot, xx, :, cols]

    def weights_y_done():
        has = member(z)
        at_slot = slot(jnp.where(has, z, twin(z)))
        cols = pl.ds(pl.multiple_of(jnp.where(has, 0, KP), 128), KP)
        for i in range(NY):
            yy = lax.rem(y + i, NY)
            rows = pl.ds(pl.multiple_of(16 * yy, 16), 16)
            recv(wb.at[at_slot, x, rows, cols], yg_r.at[yy], jnp.logical_not(has) if i == 0 else None)

    def weights_x_send():
        for i in range(1, NX):
            xx = lax.rem(x + i, NX)
            block = block_of(z, x, KZ, KX)
            send(block, block, xa_s.at[i - 1], xa_r.at[x], at(z, xx))

    def weights_x_done(i):
        xx = lax.rem(x + i, NX)
        recv(block_of(z, xx, KZ, KX), xa_r.at[xx])

    def ring(zz, d, n):
        return lax.rem(zz + (n if d == 0 else NZ - n), NZ)

    def ring_x(d, s, i):
        xx = lax.rem(x + i, NX)
        block = block_of(ring(z, 1 - d, s), xx, KZ, KX)
        last = i // 2 == d
        if s > 0 and (s < 4 or last):
            recv(block, zx_r.at[d, s - 1, xx])
        if s < 3 or (s == 3 and last):
            send(block, block, zx_s.at[d, s, xx], zx_r.at[d, s, xx], at(ring(z, d, 1), x))

    def ring_z(d, s):
        source = ring(z, 1 - d, s)
        start, size = ZHALF[d] if s == 4 else (0, KZ)
        block = block_of(source, x, start, size)
        if s > 0:
            recv(block, zz_r.at[d, s - 1])
        if s < 4:
            start, size = ZHALF[d] if s == 3 else (0, KZ)
            part = block_of(source, x, start, size)
            send(part, part, zz_s.at[d, s], zz_r.at[d, s], at(ring(z, d, 1), x))
        if s > 0 or d == 0:
            for k in range(2):
                send(block, block, xz_s.at[d, s, k], xz_r.at[d, s, k], at(z, beside(k)))

    def beside(k, n=1):
        return lax.rem(x + (n if k == 0 else NX - n), NX)

    def relay_z(d, s):
        if s == 0 and d == 1:
            return
        source = ring(z, 1 - d, s)
        start, size = ZHALF[d] if s == 4 else (0, KZ)
        for k in range(2):
            recv(block_of(source, beside(1 - k), start, size), xz_r.at[d, s, k])
            half = block_of(source, beside(1 - k), start + k * (size // 2), size // 2)
            send(half, half, xz_s.at[d, s, 2 + k], xz_r.at[d, s, 2 + k], at(z, beside(k)))

    def ring_z_done(d, s):
        if s == 0 and d == 1:
            return
        source = ring(z, 1 - d, s)
        start, size = ZHALF[d] if s == 4 else (0, KZ)
        for k in range(2):
            recv(block_of(source, beside(1 - k, 2), start + k * (size // 2), size // 2), xz_r.at[d, s, 2 + k])

    def weights_split():
        def one(i, carry):
            zi, xx = lax.div(i, NX), lax.rem(i, NX)
            high, low = split(wb[zi, xx])
            rows = pl.ds(pl.multiple_of(i * 64, 64), 64)
            wh[rows, :] = high
            wl[rows, :] = low
            return carry

        lax.fori_loop(0, 16, one, 0)

    def keys(h):
        cols = slice(h * HD, (h + 1) * HD)
        kf = features(k_ref[:, cols], km_ref[h])
        high, low = split(kf)
        kfh[h] = high
        kfl[h] = low
        st[h, 0:HD, :] = dot3(split(v_ref[:, cols].T), (high, low), NN)
        st[h, HD:SROWS, :] = jnp.broadcast_to(jnp.sum(kf, axis=0, keepdims=True), (SROWS - HD, FEAT))
        j = h % 4
        send(st.at[h], sp.at[j], dd_s.at[j], dd_r.at[j], (other, y), core != h // 4)

    def queries(h):
        cols = slice(h * HD, (h + 1) * HD)
        qf = split(features(q_ref[:, cols], qm_ref[h]))
        qfh[h], qfl[h] = qf
        w = dot3(qf, (kfh[h], kfl[h]), NT)
        causal = lax.broadcasted_iota(jnp.int32, (ROWS, ROWS), 0) >= lax.broadcasted_iota(jnp.int32, (ROWS, ROWS), 1)
        w = jnp.where(causal, w, 0.0)
        dl[h] = jnp.broadcast_to(jnp.sum(w, axis=1, keepdims=True), (ROWS, HD))
        nl[h] = dot3(split(w), split(v_ref[:, cols]), NN)

    def chip_sum(j):
        h = 4 * core + j
        recv(sp.at[j], dd_r.at[j])
        su[j] = st[h] + sp[j]
        send(su.at[j], rr.at[x], aa_s.at[j], aa_r.at[x], at(z, j), x != j)

        @pl.when(x == j)
        def _():
            rr[j] = su[j]

    def row_sum():
        for i in range(1, NX):
            xx = lax.rem(x + i, NX)
            recv(rr.at[xx], aa_r.at[xx])
        total = jnp.zeros((SROWS, FEAT), F32)
        for i in range(NX):
            bk[i] = total
            total = total + rr[i]
        for j in range(NZ):
            zt[j, 0:PIECE, :] = total[j * PIECE : (j + 1) * PIECE]
            zt[j, PIECE:, :] = total[HD:]
        for i in range(1, NZ):
            zz = lax.rem(z + i, NZ)
            send(zt.at[zz], zr.at[z], z1_s.at[i - 1], z1_r.at[z], at(zz, x))
        zr[z] = zt[z]

    def z_sum():
        for i in range(1, NZ):
            zz = lax.rem(z + i, NZ)
            recv(zr.at[zz], z1_r.at[zz])
        total = jnp.zeros((PIECE, FEAT), F32)
        norm = jnp.zeros((SROWS - HD, FEAT), F32)
        for j in range(NZ):
            zb[j] = total
            total = total + zr[j, 0:PIECE, :]
            norm = norm + jnp.where(j < z, zr[j, PIECE:, :], 0.0)
        rows = pl.ds(pl.multiple_of(z * PIECE, PIECE), PIECE)
        for i in range(1, NZ):
            zz = lax.rem(z + i, NZ)
            send(zb.at[zz], zp.at[rows, :], z2_s.at[i - 1], z2_r.at[z], at(zz, x))
        zp[rows, :] = zb[z]
        zp[HD:SROWS, :] = norm

    def send_back():
        for i in range(1, NZ):
            zz = lax.rem(z + i, NZ)
            recv(zp.at[pl.ds(pl.multiple_of(zz * PIECE, PIECE), PIECE), :], z2_r.at[zz])
        before = zp[...]
        for i in range(NX):
            bk[i] += before
            send(bk.at[i], pc.at[x], bb_s.at[i], bb_r.at[x], at(z, i), x != i)

            @pl.when(x == i)
            def _(i=i):
                pc[i] = bk[i]

    def cores_prefix():
        for j in range(4):
            if j == 0:
                for i in range(1, NX):
                    xx = lax.rem(x + i, NX)
                    recv(pc.at[xx], bb_r.at[xx])
            h = 4 * core + j
            low = pc[j]
            high = low + jnp.where(core == 0, st[h], sp[j])
            pf[h] = jnp.where(core == 0, low, high)
            sd[j] = jnp.where(core == 0, high, low)
            send(sd.at[j], pf.at[h], ee_s.at[j], ee_r.at[j], (other, y))

    def prefix_done():
        for j in range(4):
            recv(pf.at[4 * (1 - core) + j], ee_r.at[j])

    def mix(c):
        rows = pl.ds(c * CR, CR)
        for h in range(HEADS):
            state = pf[h]
            qf = (qfh[h, c * CR : (c + 1) * CR, :], qfl[h, c * CR : (c + 1) * CR, :])
            far_sum = dot3(qf, split(state), NT)
            denom = dl[h, c * CR : (c + 1) * CR, :] + far_sum[:, HD : HD + 1]
            ab[yp, core, rows, h * HD : (h + 1) * HD] = (nl[h, c * CR : (c + 1) * CR, :] + far_sum[:, :HD]) / denom
        block = ab.at[yp, core, rows, :]
        send(block, block, m_s.at[c, 0], m_r.at[c, 0], (ctx, pair))
        send(block, block, m_s.at[c, 1], m_r.at[c, 1], (other, y))

    def relay(c):
        rows = pl.ds(c * CR, CR)
        block = ab.at[1 - yp, core, rows, :]
        recv(block, m_r.at[c, 0])
        send(block, block, m_s.at[c, 2], m_r.at[c, 2], (other, y))

    def project(c):
        rows = pl.ds(c * CR, CR)
        recv(ab.at[yp, 1 - core, rows, :], m_r.at[c, 1])
        recv(ab.at[1 - yp, 1 - core, rows, :], m_r.at[c, 2])
        for cc in range(2):
            for yy in range(2):
                high, low = split(ab[yy, cc, c * CR : (c + 1) * CR, :])
                ah[cc * CR : (cc + 1) * CR, yy * WIDTH : (yy + 1) * WIDTH] = high
                al[cc * CR : (cc + 1) * CR, yy * WIDTH : (yy + 1) * WIDTH] = low
        for base, dst in ((512, cs), (0, co)):

            def one(n, carry, base=base, dst=dst):
                wrows = pl.ds(pl.multiple_of(base + n * 256, 256), 256)
                cols = pl.ds(pl.multiple_of(n * 256, 256), 256)
                dst[c, :, cols] = dot3((ah[...], al[...]), (wh[wrows, :], wl[wrows, :]), NT)
                return carry

            lax.fori_loop(0, 2, one, 0)
            if base:
                send(cs.at[c], cr.at[c], c_s.at[c], c_r.at[c], (ctx, far))

    def gather(c):
        recv(cr.at[c], c_r.at[c])
        co[c] += cr[c]
        theirs = co.at[c, pl.ds(pl.multiple_of((1 - core) * CR, CR), CR), :]
        send(theirs, fr.at[c], f_s.at[c], f_r.at[c], (other, y))

    def finish(c):
        recv(fr.at[c], f_r.at[c])
        low_half = lax.broadcasted_iota(jnp.int32, (CR, 128), 1) < 64
        for cc in range(2):

            @pl.when(core == cc)
            def _(cc=cc):
                for m in range(4):
                    cols = slice(m * 128, (m + 1) * 128)
                    a, b = co[c, cc * CR : (cc + 1) * CR, cols], fr[c, :, cols]
                    if cc:
                        a, b = b, a
                    out_ref[c * CR : (c + 1) * CR, m * 256 : m * 256 + 128] = jnp.where(low_half, a, pltpu.roll(b, 64, 1))
                    out_ref[c * CR : (c + 1) * CR, m * 256 + 128 : (m + 1) * 256] = jnp.where(
                        low_half, pltpu.roll(a, 64, 1), b
                    )

    def ring_unit(s, i):
        for d in range(2):
            ring_x(d, s, i)
        if i == 0:
            for d in range(2):
                ring_z(d, s)
        if i == 2:
            for d in range(2):
                relay_z(d, s - 1)

    units = [(s, i) for s in range(1, 5) for i in range(NX)]

    def advance(n):
        for _ in range(n):
            if units:
                ring_unit(*units.pop(0))

    for j in range(4):
        keys(j)
        keys(4 + j)
        if j > 0:
            chip_sum(j - 1)
    chip_sum(3)
    weights_y_done()
    weights_x_send()
    for d in range(2):
        ring_x(d, 0, 0)
        ring_z(d, 0)
    for h in range(4):
        queries(h)
    row_sum()
    for i in range(1, NX):
        weights_x_done(i)
        for d in range(2):
            ring_x(d, 0, i)
    for h in range(4, HEADS):
        queries(h)
    advance(2)
    z_sum()
    advance(2)
    send_back()
    advance(3)
    cores_prefix()
    advance(1)
    prefix_done()
    for c in range(CHUNKS):
        mix(c)
        advance(1)
    advance(1)
    relay(0)
    advance(2)
    relay(1)
    advance(16)
    for d in range(2):
        relay_z(d, 4)
    relay(2)
    for s in range(5):
        for d in range(2):
            ring_z_done(d, s)
    weights_split()
    for c in range(CHUNKS):
        project(c)
        if c == 0:
            relay(3)
        if c > 1:
            gather(c - 2)
    gather(CHUNKS - 2)
    for c in range(CHUNKS - 1):
        finish(c)
    gather(CHUNKS - 1)
    finish(CHUNKS - 1)
    for when, c in pending:
        if when is None:
            c.wait_send()
        else:
            pl.when(when)(c.wait_send)


def attend(q, k, v, qm, km, wt):
    dma = pltpu.SemaphoreType.DMA
    vmem = pltpu.VMEM
    scratch = [
        vmem((HEADS, ROWS, FEAT), BF16), vmem((HEADS, ROWS, FEAT), BF16),
        vmem((HEADS, ROWS, FEAT), BF16), vmem((HEADS, ROWS, FEAT), BF16),
        vmem((HEADS, ROWS, HD), F32), vmem((HEADS, ROWS, HD), F32),
        vmem((HEADS, SROWS, FEAT), F32), vmem((4, SROWS, FEAT), F32), vmem((4, SROWS, FEAT), F32),
        vmem((NX, SROWS, FEAT), F32), vmem((NX, SROWS, FEAT), F32), vmem((NX, SROWS, FEAT), F32),
        vmem((4, SROWS, FEAT), F32), vmem((HEADS, SROWS, FEAT), F32),
        vmem((NZ, PIECE + 8, FEAT), F32), vmem((NZ, PIECE + 8, FEAT), F32),
        vmem((NZ, PIECE, FEAT), F32), vmem((SROWS, FEAT), F32),
        vmem((4, NX, 64, HALF), F32), vmem((1024, HALF), BF16), vmem((1024, HALF), BF16),
        vmem((2, 2, ROWS, WIDTH), F32), vmem((2 * CR, HALF), BF16), vmem((2 * CR, HALF), BF16),
        vmem((CHUNKS, 2 * CR, 512), F32), vmem((CHUNKS, 2 * CR, 512), F32),
        vmem((CHUNKS, 2 * CR, 512), F32), vmem((CHUNKS, CR, 512), F32),
        dma((2, 2)), dma((NY,)), dma((3,)), dma((NX,)),
        dma((2, 4, NX)), dma((2, 4, NX)), dma((2, 4)), dma((2, 4)),
        dma((2, 5, 4)), dma((2, 5, 4)),
        dma((4,)), dma((4,)), dma((4,)), dma((NX,)), dma((NZ - 1,)), dma((NZ,)), dma((NZ - 1,)), dma((NZ,)),
        dma((4,)), dma((NX,)), dma((4,)), dma((4,)),
        dma((CHUNKS, 3)), dma((CHUNKS, 3)), dma((CHUNKS,)), dma((CHUNKS,)), dma((CHUNKS,)), dma((CHUNKS,)),
    ]
    return pl.pallas_call(
        kernel,
        out_shape=jax.ShapeDtypeStruct((ROWS, WIDTH), F32),
        in_specs=[pl.BlockSpec(memory_space=vmem)] * 6,
        out_specs=pl.BlockSpec(memory_space=vmem),
        scratch_shapes=scratch,
        compiler_params=pltpu.CompilerParams(
            collective_id=0, has_side_effects=True, vmem_limit_bytes=60 * 1024 * 1024
        ),
    )(q, k, v, qm, km, wt)


def body(queries, keys, values, query_map, key_map, out_weight, residual):
    return residual + attend(queries, keys, values, query_map, key_map, out_weight.T)


def solution(mesh):
    placed = (
        P("ctx", "head"),
        P("ctx", "head"),
        P("ctx", "head"),
        P("head", None, None),
        P("head", None, None),
        P(None, ("ctx", "head")),
        P("ctx", "head"),
    )
    return jax.shard_map(body, mesh=mesh, in_specs=placed, out_specs=P("ctx", "head"), check_vma=False)
```

```python
import jax
import jax.numpy as jnp
from jax import lax
from jax.experimental import pallas as pl
from jax.experimental.pallas import tpu as pltpu
from jax.sharding import PartitionSpec as P

MESH = pl.DeviceIdType.MESH
NX, NY, NZ = 4, 4, 8
ROWS, HEADS, HD, FEAT = 256, 8, 128, 256
WIDTH = HEADS * HD
KP = 1024
KZ = 512
KX = KP - KZ
ZHALF = ((0, 256), (256, 256))
PIECE = 16
SROWS = 136
CHUNKS = 4
CR = ROWS // CHUNKS
F32, BF16 = jnp.float32, jnp.bfloat16

NN = (((1,), (0,)), ((), ()))
NT = (((1,), (1,)), ((), ()))


def split(a):
    high = a.astype(BF16)
    return high, (a - high.astype(F32)).astype(BF16)


def dot3(a, b, dims):
    (ah, al), (bh, bl) = a, b

    def one(p, q):
        return lax.dot_general(p, q, dims, preferred_element_type=F32)

    return one(ah, bh) + (one(ah, bl) + one(al, bh))


def features(inputs, weights):
    s = dot3(split(inputs), split(weights), NN)
    up = jnp.exp(s - jnp.max(s, axis=1, keepdims=True))
    down = jnp.exp(jnp.min(s, axis=1, keepdims=True) - s)
    up = up / jnp.sum(up, axis=1, keepdims=True)
    down = down / jnp.sum(down, axis=1, keepdims=True)
    return jnp.concatenate([up, down], axis=1)


def kernel(
    q_ref, k_ref, v_ref, qm_ref, km_ref, wt_ref, out_ref,
    qfh, qfl, kfh, kfl, nl, dl, st, sp, su, rr, bk, pc, sd, pf, zt, zr, zb, zp,
    wb, wh, wl, ab, ah, al, co, fr,
    yg_s, yg_r, xa_s, xa_r, zx_s, zx_r, zz_s, zz_r, xz_s, xz_r,
    dd_s, dd_r, aa_s, aa_r, z1_s, z1_r, z2_s, z2_r, bb_s, bb_r, ee_s, ee_r, m_s, m_r, f_s, f_r,
):
    ctx, y = lax.axis_index("ctx"), lax.axis_index("head")
    core, r = lax.rem(ctx, 2), lax.rem(ctx, 8)
    x, z = lax.div(r, 2), lax.div(ctx, 8)
    other = ctx + 1 - 2 * core
    pending = []

    def at(zz, xx):
        return ((zz * NX + xx) * 2 + core, y)

    def copy(src, dst, send, recv, device):
        return pltpu.make_async_remote_copy(
            src_ref=src, dst_ref=dst, send_sem=send, recv_sem=recv, device_id=device, device_id_type=MESH
        )

    def send(src, dst, ss, rs, device, when=None):
        c = copy(src, dst, ss, rs, device)
        if when is None:
            c.start()
        else:
            pl.when(when)(c.start)
        pending.append((when, c))

    def recv(dst, rs, when=None):
        c = copy(dst, dst, rs, rs, (ctx, y))
        if when is None:
            c.wait_recv()
        else:
            pl.when(when)(c.wait_recv)

    barrier = pltpu.get_barrier_semaphore()
    greeted = [(ctx, lax.rem(y + i, NY)) for i in range(1, NY)]
    greeted += [at(z, lax.rem(x + i, NX)) for i in range(1, NX)] + [(other, y)]
    greeted += [at(lax.rem(z + i, NZ), x) for i in range(1, NZ)]
    for device in greeted:
        pl.semaphore_signal(barrier, inc=1, device_id=device, device_id_type=MESH)
    parity, zy = lax.rem(z, 2), lax.div(z, 2)
    for i in range(NY):
        to_there = at(2 * i + parity, x)[0]

        @pl.when(jnp.logical_or(i != zy, y != zy))
        def _(there=to_there):
            pl.semaphore_signal(barrier, inc=1, device_id=(there, zy), device_id_type=MESH)

        @pl.when(jnp.logical_or(i != y, y != zy))
        def _(i=i):
            pl.semaphore_signal(barrier, inc=1, device_id=(at(2 * y + parity, x)[0], i), device_id_type=MESH)

    pl.semaphore_wait(barrier, len(greeted) + jnp.where(y == zy, 6, 8))

    my_rows = pl.ds(pl.multiple_of(16 * y, 16), 16)
    for i in range(NY):
        cols = pl.ds(i * KP, KP)
        away = jnp.logical_or(i != zy, y != zy)
        dst = wb.at[parity, x, my_rows, cols]
        send(wt_ref.at[:, cols], dst, yg_s.at[i], yg_r.at[y], (at(2 * i + parity, x)[0], zy), away)

        @pl.when(jnp.logical_not(away))
        def _(i=i):
            wb[parity, x, my_rows, i * KP : (i + 1) * KP] = wt_ref[:, i * KP : (i + 1) * KP]

    def block_of(zz, xx, start, size):
        cols = pl.ds(pl.multiple_of(KP * lax.div(zz, 2) + start, 128), size)
        return wb.at[lax.rem(zz, 2), xx, :, cols]

    def weights_y_done():
        cols = pl.ds(pl.multiple_of(KP * zy, KP), KP)
        for i in range(NY):
            rows = pl.ds(16 * i, 16)
            recv(wb.at[parity, x, rows, cols], yg_r.at[i], jnp.logical_or(i != y, y != zy))

    def weights_x_send():
        for i in range(1, NX):
            xx = lax.rem(x + i, NX)
            block = block_of(z, x, KZ, KX)
            send(block, block, xa_s.at[i - 1], xa_r.at[x], at(z, xx))

    def weights_x_done(i):
        xx = lax.rem(x + i, NX)
        recv(block_of(z, xx, KZ, KX), xa_r.at[xx])

    def ring(zz, d, n):
        return lax.rem(zz + (n if d == 0 else NZ - n), NZ)

    def ring_x(d, s, i):
        xx = lax.rem(x + i, NX)
        block = block_of(ring(z, 1 - d, s), xx, KZ, KX)
        last = i // 2 == d
        if s > 0 and (s < 4 or last):
            recv(block, zx_r.at[d, s - 1, xx])
        if s < 3 or (s == 3 and last):
            send(block, block, zx_s.at[d, s, xx], zx_r.at[d, s, xx], at(ring(z, d, 1), x))

    def ring_z(d, s):
        source = ring(z, 1 - d, s)
        start, size = ZHALF[d] if s == 4 else (0, KZ)
        block = block_of(source, x, start, size)
        if s > 0:
            recv(block, zz_r.at[d, s - 1])
        if s < 4:
            start, size = ZHALF[d] if s == 3 else (0, KZ)
            part = block_of(source, x, start, size)
            send(part, part, zz_s.at[d, s], zz_r.at[d, s], at(ring(z, d, 1), x))
        if s > 0 or d == 0:
            for k in range(2):
                send(block, block, xz_s.at[d, s, k], xz_r.at[d, s, k], at(z, beside(k)))

    def beside(k, n=1):
        return lax.rem(x + (n if k == 0 else NX - n), NX)

    def part_of(start, size, k):
        cut = size // 256 * 128
        return (start, cut) if k == 0 else (start + cut, size - cut)

    def relay_z(d, s):
        if s == 0 and d == 1:
            return
        source = ring(z, 1 - d, s)
        start, size = ZHALF[d] if s == 4 else (0, KZ)
        for k in range(2):
            recv(block_of(source, beside(1 - k), start, size), xz_r.at[d, s, k])
            half = block_of(source, beside(1 - k), *part_of(start, size, k))
            send(half, half, xz_s.at[d, s, 2 + k], xz_r.at[d, s, 2 + k], at(z, beside(k)))

    def ring_z_done(d, s):
        if s == 0 and d == 1:
            return
        source = ring(z, 1 - d, s)
        start, size = ZHALF[d] if s == 4 else (0, KZ)
        for k in range(2):
            recv(block_of(source, beside(1 - k, 2), *part_of(start, size, k)), xz_r.at[d, s, 2 + k])

    def weights_split():
        def one(i, carry):
            high, low = split(wb[lax.div(i, NX), lax.rem(i, NX)])
            rows = pl.ds(pl.multiple_of(i * 64, 64), 64)
            wh[rows, :] = high
            wl[rows, :] = low
            return carry

        lax.fori_loop(0, 8, one, 0)

    def keys(h):
        cols = slice(h * HD, (h + 1) * HD)
        kf = features(k_ref[:, cols], km_ref[h])
        high, low = split(kf)
        kfh[h] = high
        kfl[h] = low
        st[h, 0:HD, :] = dot3(split(v_ref[:, cols].T), (high, low), NN)
        st[h, HD:SROWS, :] = jnp.broadcast_to(jnp.sum(kf, axis=0, keepdims=True), (SROWS - HD, FEAT))
        j = h % 4
        send(st.at[h], sp.at[j], dd_s.at[j], dd_r.at[j], (other, y), core != h // 4)

    def queries(h):
        cols = slice(h * HD, (h + 1) * HD)
        qf = split(features(q_ref[:, cols], qm_ref[h]))
        qfh[h], qfl[h] = qf
        w = dot3(qf, (kfh[h], kfl[h]), NT)
        causal = lax.broadcasted_iota(jnp.int32, (ROWS, ROWS), 0) >= lax.broadcasted_iota(jnp.int32, (ROWS, ROWS), 1)
        w = jnp.where(causal, w, 0.0)
        dl[h] = jnp.broadcast_to(jnp.sum(w, axis=1, keepdims=True), (ROWS, HD))
        nl[h] = dot3(split(w), split(v_ref[:, cols]), NN)

    def chip_sum(j):
        h = 4 * core + j
        recv(sp.at[j], dd_r.at[j])
        su[j] = st[h] + sp[j]
        send(su.at[j], rr.at[x], aa_s.at[j], aa_r.at[x], at(z, j), x != j)

        @pl.when(x == j)
        def _():
            rr[j] = su[j]

    def row_sum():
        for i in range(1, NX):
            xx = lax.rem(x + i, NX)
            recv(rr.at[xx], aa_r.at[xx])
        total = jnp.zeros((SROWS, FEAT), F32)
        for i in range(NX):
            bk[i] = total
            total = total + rr[i]
        for j in range(NZ):
            zt[j, 0:PIECE, :] = total[j * PIECE : (j + 1) * PIECE]
            zt[j, PIECE:, :] = total[HD:]
        for i in range(1, NZ):
            zz = lax.rem(z + i, NZ)
            send(zt.at[zz], zr.at[z], z1_s.at[i - 1], z1_r.at[z], at(zz, x))
        zr[z] = zt[z]

    def z_sum():
        for i in range(1, NZ):
            zz = lax.rem(z + i, NZ)
            recv(zr.at[zz], z1_r.at[zz])
        total = jnp.zeros((PIECE, FEAT), F32)
        norm = jnp.zeros((SROWS - HD, FEAT), F32)
        for j in range(NZ):
            zb[j] = total
            total = total + zr[j, 0:PIECE, :]
            norm = norm + jnp.where(j < z, zr[j, PIECE:, :], 0.0)
        rows = pl.ds(pl.multiple_of(z * PIECE, PIECE), PIECE)
        for i in range(1, NZ):
            zz = lax.rem(z + i, NZ)
            send(zb.at[zz], zp.at[rows, :], z2_s.at[i - 1], z2_r.at[z], at(zz, x))
        zp[rows, :] = zb[z]
        zp[HD:SROWS, :] = norm

    def send_back():
        for i in range(1, NZ):
            zz = lax.rem(z + i, NZ)
            recv(zp.at[pl.ds(pl.multiple_of(zz * PIECE, PIECE), PIECE), :], z2_r.at[zz])
        before = zp[...]
        for i in range(NX):
            bk[i] += before
            send(bk.at[i], pc.at[x], bb_s.at[i], bb_r.at[x], at(z, i), x != i)

            @pl.when(x == i)
            def _(i=i):
                pc[i] = bk[i]

    def cores_prefix():
        for j in range(4):
            if j == 0:
                for i in range(1, NX):
                    xx = lax.rem(x + i, NX)
                    recv(pc.at[xx], bb_r.at[xx])
            h = 4 * core + j
            low = pc[j]
            high = low + jnp.where(core == 0, st[h], sp[j])
            pf[h] = jnp.where(core == 0, low, high)
            sd[j] = jnp.where(core == 0, high, low)
            send(sd.at[j], pf.at[h], ee_s.at[j], ee_r.at[j], (other, y))

    def prefix_done():
        for j in range(4):
            recv(pf.at[4 * (1 - core) + j], ee_r.at[j])

    def mix(c):
        rows = pl.ds(c * CR, CR)
        for h in range(HEADS):
            state = pf[h]
            qf = (qfh[h, c * CR : (c + 1) * CR, :], qfl[h, c * CR : (c + 1) * CR, :])
            far_sum = dot3(qf, split(state), NT)
            denom = dl[h, c * CR : (c + 1) * CR, :] + far_sum[:, HD : HD + 1]
            ab[y, core, rows, h * HD : (h + 1) * HD] = (nl[h, c * CR : (c + 1) * CR, :] + far_sum[:, :HD]) / denom
        block = ab.at[y, core, rows, :]
        for k in range(2):
            send(block, block, m_s.at[c, k], m_r.at[c, k], (ctx, next_y(k)))
        send(block, block, m_s.at[c, 2], m_r.at[c, 4], (other, y))

    def next_y(k, n=1):
        return lax.rem(y + (n if k == 0 else NY - n), NY)

    def relay(c):
        for k in range(2):
            yy = next_y(1 - k)
            block = ab.at[yy, core, pl.ds(c * CR, CR), :]
            recv(block, m_r.at[c, k])
            half = ab.at[yy, core, pl.ds(c * CR + k * (CR // 2), CR // 2), :]
            send(half, half, m_s.at[c, 3 + k], m_r.at[c, 2 + k], (ctx, next_y(k)))
            send(block, block, m_s.at[c, 5 + k], m_r.at[c, 5 + k], (other, y))

    def relay_far(c):
        yy = next_y(0, 2)
        for k in range(2):
            recv(ab.at[yy, core, pl.ds(c * CR + k * (CR // 2), CR // 2), :], m_r.at[c, 2 + k])
        block = ab.at[yy, core, pl.ds(c * CR, CR), :]
        send(block, block, m_s.at[c, 7], m_r.at[c, 7], (other, y))

    def gather(c):
        for k, yy in enumerate((y, next_y(1), next_y(0), next_y(0, 2))):
            recv(ab.at[yy, 1 - core, pl.ds(c * CR, CR), :], m_r.at[c, 4 + k])
        for cc in range(2):
            for yy in range(NY):
                high, low = split(ab[yy, cc, c * CR : (c + 1) * CR, :])
                rows, cols = slice(cc * ROWS + c * CR, cc * ROWS + (c + 1) * CR), slice(yy * WIDTH, (yy + 1) * WIDTH)
                ah[rows, cols] = high
                al[rows, cols] = low

    def project(n, m):
        owner = core if m == 0 else 1 - core
        rows = pl.ds(pl.multiple_of(owner * ROWS, ROWS), ROWS)
        wrows = slice(n * 256, (n + 1) * 256)
        co[n, m] = dot3((ah[rows, :], al[rows, :]), (wh[wrows, :], wl[wrows, :]), NT)
        if m:
            send(co.at[n, 1], fr.at[n], f_s.at[n], f_r.at[n], (other, y))

    def finish(n):
        recv(fr.at[n], f_r.at[n])
        low_half = lax.broadcasted_iota(jnp.int32, (ROWS, 128), 1) < 64
        for cc in range(2):

            @pl.when(core == cc)
            def _(cc=cc):
                for m in range(2):
                    cols = slice(m * 128, (m + 1) * 128)
                    a, b = co[n, 0, :, cols], fr[n, :, cols]
                    if cc:
                        a, b = b, a
                    start = n * 512 + m * 256
                    out_ref[:, start : start + 128] = jnp.where(low_half, a, pltpu.roll(b, 64, 1))
                    out_ref[:, start + 128 : start + 256] = jnp.where(low_half, pltpu.roll(a, 64, 1), b)

    def ring_unit(s, i):
        for d in range(2):
            ring_x(d, s, i)
        if i == 0:
            for d in range(2):
                ring_z(d, s)
        if i == 2:
            for d in range(2):
                relay_z(d, s - 1)

    units = [(s, i) for s in range(1, 5) for i in range(NX)]

    def advance(n):
        for _ in range(n):
            if units:
                ring_unit(*units.pop(0))

    for j in range(4):
        keys(j)
        keys(4 + j)
        if j > 0:
            chip_sum(j - 1)
    chip_sum(3)
    weights_y_done()
    weights_x_send()
    for d in range(2):
        ring_x(d, 0, 0)
        ring_z(d, 0)
    for h in range(0, 4):
        queries(h)
    row_sum()
    for h in range(4, 8):
        queries(h)
    z_sum()
    for i in range(1, NX):
        weights_x_done(i)
        for d in range(2):
            ring_x(d, 0, i)
    send_back()
    advance(2)
    cores_prefix()
    advance(1)
    prefix_done()
    for c in range(CHUNKS):
        mix(c)
    advance(1)
    relay(0)
    advance(2)
    relay(1)
    advance(2)
    relay(2)
    advance(2)
    relay(3)
    advance(1)
    relay_far(0)
    advance(1)
    relay_far(1)
    gather(0)
    advance(1)
    relay_far(2)
    gather(1)
    relay_far(3)
    advance(16)
    gather(2)
    for d in range(2):
        relay_z(d, 4)
    for s in range(5):
        for d in range(2):
            ring_z_done(d, s)
    gather(3)
    weights_split()
    for n in range(2):
        project(n, 1)
        project(n, 0)
        if n:
            finish(0)
    finish(1)
    for when, c in pending:
        if when is None:
            c.wait_send()
        else:
            pl.when(when)(c.wait_send)


def attend(q, k, v, qm, km, wt):
    dma = pltpu.SemaphoreType.DMA
    vmem = pltpu.VMEM
    scratch = [
        vmem((HEADS, ROWS, FEAT), BF16), vmem((HEADS, ROWS, FEAT), BF16),
        vmem((HEADS, ROWS, FEAT), BF16), vmem((HEADS, ROWS, FEAT), BF16),
        vmem((HEADS, ROWS, HD), F32), vmem((HEADS, ROWS, HD), F32),
        vmem((HEADS, SROWS, FEAT), F32), vmem((4, SROWS, FEAT), F32), vmem((4, SROWS, FEAT), F32),
        vmem((NX, SROWS, FEAT), F32), vmem((NX, SROWS, FEAT), F32), vmem((NX, SROWS, FEAT), F32),
        vmem((4, SROWS, FEAT), F32), vmem((HEADS, SROWS, FEAT), F32),
        vmem((NZ, PIECE + 8, FEAT), F32), vmem((NZ, PIECE + 8, FEAT), F32),
        vmem((NZ, PIECE, FEAT), F32), vmem((SROWS, FEAT), F32),
        vmem((2, NX, 64, NY * WIDTH), F32), vmem((512, NY * WIDTH), BF16), vmem((512, NY * WIDTH), BF16),
        vmem((NY, 2, ROWS, WIDTH), F32), vmem((2 * ROWS, NY * WIDTH), BF16), vmem((2 * ROWS, NY * WIDTH), BF16),
        vmem((2, 2, ROWS, 256), F32), vmem((2, ROWS, 256), F32),
        dma((NY,)), dma((NY,)), dma((3,)), dma((NX,)),
        dma((2, 4, NX)), dma((2, 4, NX)), dma((2, 4)), dma((2, 4)),
        dma((2, 5, 4)), dma((2, 5, 4)),
        dma((4,)), dma((4,)), dma((4,)), dma((NX,)), dma((NZ - 1,)), dma((NZ,)), dma((NZ - 1,)), dma((NZ,)),
        dma((4,)), dma((NX,)), dma((4,)), dma((4,)),
        dma((CHUNKS, 8)), dma((CHUNKS, 8)), dma((2,)), dma((2,)),
    ]
    return pl.pallas_call(
        kernel,
        out_shape=jax.ShapeDtypeStruct((ROWS, WIDTH), F32),
        in_specs=[pl.BlockSpec(memory_space=vmem)] * 6,
        out_specs=pl.BlockSpec(memory_space=vmem),
        scratch_shapes=scratch,
        compiler_params=pltpu.CompilerParams(
            collective_id=0, has_side_effects=True, vmem_limit_bytes=60 * 1024 * 1024
        ),
    )(q, k, v, qm, km, wt)


def body(queries, keys, values, query_map, key_map, out_weight, residual):
    return residual + attend(queries, keys, values, query_map, key_map, out_weight.T)


def solution(mesh):
    placed = (
        P("ctx", "head"),
        P("ctx", "head"),
        P("ctx", "head"),
        P("head", None, None),
        P("head", None, None),
        P(None, ("ctx", "head")),
        P("ctx", "head"),
    )
    return jax.shard_map(body, mesh=mesh, in_specs=placed, out_specs=P("ctx", "head"), check_vma=False)
```

```python
import jax
import jax.numpy as jnp
from jax import lax
from jax.experimental import pallas as pl
from jax.experimental.pallas import tpu as pltpu
from jax.sharding import PartitionSpec as P

MESH = pl.DeviceIdType.MESH
NX, NY, NZ = 4, 4, 8
ROWS, HEADS, HD, FEAT = 256, 8, 128, 256
WIDTH = HEADS * HD
KP = 1024
KZ = 512
KX = KP - KZ
ZHALF = ((0, 256), (256, 256))
PIECE = 16
SROWS = 136
CHUNKS = 4
CR = ROWS // CHUNKS
F32, BF16 = jnp.float32, jnp.bfloat16

NN = (((1,), (0,)), ((), ()))
NT = (((1,), (1,)), ((), ()))


def split(a):
    high = a.astype(BF16)
    return high, (a - high.astype(F32)).astype(BF16)


def dot3(a, b, dims):
    (ah, al), (bh, bl) = a, b

    def one(p, q):
        return lax.dot_general(p, q, dims, preferred_element_type=F32)

    return one(ah, bh) + (one(ah, bl) + one(al, bh))


def features(inputs, weights):
    s = dot3(split(inputs), split(weights), NN)
    up = jnp.exp(s - jnp.max(s, axis=1, keepdims=True))
    down = jnp.exp(jnp.min(s, axis=1, keepdims=True) - s)
    up = up / jnp.sum(up, axis=1, keepdims=True)
    down = down / jnp.sum(down, axis=1, keepdims=True)
    return jnp.concatenate([up, down], axis=1)


def kernel(
    q_in, k_in, v_in, qm_in, km_in, wt_in, res_in, out_ref,
    q_ref, k_ref, v_ref, qm_ref, km_ref, wt_ref, res_ref,
    qfh, qfl, kfh, kfl, nl, dl, st, sp, su, rr, bk, pc, sd, pf, zt, zr, zb, zp,
    wb, wh, wl, ab, ah, al, co, fr,
    yg_s, yg_r, xa_s, xa_r, zx_s, zx_r, zz_s, zz_r, xz_s, xz_r,
    dd_s, dd_r, aa_s, aa_r, z1_s, z1_r, z2_s, z2_r, bb_s, bb_r, ee_s, ee_r, m_s, m_r, f_s, f_r, in_s,
):
    ctx, y = lax.axis_index("ctx"), lax.axis_index("head")
    core, r = lax.rem(ctx, 2), lax.rem(ctx, 8)
    x, z = lax.div(r, 2), lax.div(ctx, 8)
    other = ctx + 1 - 2 * core
    pending = []
    loads = {}
    inputs = (wt_in, wt_ref), (k_in, k_ref), (km_in, km_ref), (v_in, v_ref), (q_in, q_ref), (qm_in, qm_ref), (res_in, res_ref)
    for n, (src, dst) in enumerate(inputs):
        loads[n] = pltpu.make_async_copy(src, dst, in_s.at[n])
        loads[n].start()

    def at(zz, xx):
        return ((zz * NX + xx) * 2 + core, y)

    def copy(src, dst, send, recv, device):
        return pltpu.make_async_remote_copy(
            src_ref=src, dst_ref=dst, send_sem=send, recv_sem=recv, device_id=device, device_id_type=MESH
        )

    def send(src, dst, ss, rs, device, when=None):
        c = copy(src, dst, ss, rs, device)
        if when is None:
            c.start()
        else:
            pl.when(when)(c.start)
        pending.append((when, c))

    def recv(dst, rs, when=None):
        c = copy(dst, dst, rs, rs, (ctx, y))
        if when is None:
            c.wait_recv()
        else:
            pl.when(when)(c.wait_recv)

    barrier = pltpu.get_barrier_semaphore()
    greeted = [(ctx, lax.rem(y + i, NY)) for i in range(1, NY)]
    greeted += [at(z, lax.rem(x + i, NX)) for i in range(1, NX)] + [(other, y)]
    greeted += [at(lax.rem(z + i, NZ), x) for i in range(1, NZ)]
    for device in greeted:
        pl.semaphore_signal(barrier, inc=1, device_id=device, device_id_type=MESH)
    parity, zy = lax.rem(z, 2), lax.div(z, 2)
    for i in range(NY):
        to_there = at(2 * i + parity, x)[0]

        @pl.when(jnp.logical_or(i != zy, y != zy))
        def _(there=to_there):
            pl.semaphore_signal(barrier, inc=1, device_id=(there, zy), device_id_type=MESH)

        @pl.when(jnp.logical_or(i != y, y != zy))
        def _(i=i):
            pl.semaphore_signal(barrier, inc=1, device_id=(at(2 * y + parity, x)[0], i), device_id_type=MESH)

    pl.semaphore_wait(barrier, len(greeted) + jnp.where(y == zy, 6, 8))

    loads[0].wait()

    my_rows = pl.ds(pl.multiple_of(16 * y, 16), 16)
    for i in range(NY):
        cols = pl.ds(i * KP, KP)
        away = jnp.logical_or(i != zy, y != zy)
        dst = wb.at[parity, x, my_rows, cols]
        send(wt_ref.at[:, cols], dst, yg_s.at[i], yg_r.at[y], (at(2 * i + parity, x)[0], zy), away)

        @pl.when(jnp.logical_not(away))
        def _(i=i):
            wb[parity, x, my_rows, i * KP : (i + 1) * KP] = wt_ref[:, i * KP : (i + 1) * KP]

    def block_of(zz, xx, start, size):
        cols = pl.ds(pl.multiple_of(KP * lax.div(zz, 2) + start, 128), size)
        return wb.at[lax.rem(zz, 2), xx, :, cols]

    def weights_y_done():
        cols = pl.ds(pl.multiple_of(KP * zy, KP), KP)
        for i in range(NY):
            rows = pl.ds(16 * i, 16)
            recv(wb.at[parity, x, rows, cols], yg_r.at[i], jnp.logical_or(i != y, y != zy))

    def weights_x_send():
        for i in range(1, NX):
            xx = lax.rem(x + i, NX)
            block = block_of(z, x, KZ, KX)
            send(block, block, xa_s.at[i - 1], xa_r.at[x], at(z, xx))

    def weights_x_done(i):
        xx = lax.rem(x + i, NX)
        recv(block_of(z, xx, KZ, KX), xa_r.at[xx])

    def ring(zz, d, n):
        return lax.rem(zz + (n if d == 0 else NZ - n), NZ)

    def ring_x(d, s, i):
        xx = lax.rem(x + i, NX)
        block = block_of(ring(z, 1 - d, s), xx, KZ, KX)
        last = i // 2 == d
        if s > 0 and (s < 4 or last):
            recv(block, zx_r.at[d, s - 1, xx])
        if s < 3 or (s == 3 and last):
            send(block, block, zx_s.at[d, s, xx], zx_r.at[d, s, xx], at(ring(z, d, 1), x))

    def ring_z(d, s):
        source = ring(z, 1 - d, s)
        start, size = ZHALF[d] if s == 4 else (0, KZ)
        block = block_of(source, x, start, size)
        if s > 0:
            recv(block, zz_r.at[d, s - 1])
        if s < 4:
            start, size = ZHALF[d] if s == 3 else (0, KZ)
            part = block_of(source, x, start, size)
            send(part, part, zz_s.at[d, s], zz_r.at[d, s], at(ring(z, d, 1), x))
        if s > 0 or d == 0:
            for k in range(2):
                send(block, block, xz_s.at[d, s, k], xz_r.at[d, s, k], at(z, beside(k)))

    def beside(k, n=1):
        return lax.rem(x + (n if k == 0 else NX - n), NX)

    def part_of(start, size, k):
        cut = size // 256 * 128
        return (start, cut) if k == 0 else (start + cut, size - cut)

    def relay_z(d, s):
        if s == 0 and d == 1:
            return
        source = ring(z, 1 - d, s)
        start, size = ZHALF[d] if s == 4 else (0, KZ)
        for k in range(2):
            recv(block_of(source, beside(1 - k), start, size), xz_r.at[d, s, k])
            half = block_of(source, beside(1 - k), *part_of(start, size, k))
            send(half, half, xz_s.at[d, s, 2 + k], xz_r.at[d, s, 2 + k], at(z, beside(k)))

    def ring_z_done(d, s):
        if s == 0 and d == 1:
            return
        source = ring(z, 1 - d, s)
        start, size = ZHALF[d] if s == 4 else (0, KZ)
        for k in range(2):
            recv(block_of(source, beside(1 - k, 2), *part_of(start, size, k)), xz_r.at[d, s, 2 + k])

    def weights_split(zz):
        cols = pl.ds(pl.multiple_of(KP * lax.div(zz, 2), KP), KP)
        half = lax.rem(zz, 2)

        def one(i, carry):
            high, low = split(wb[half, i, :, cols])
            rows = pl.ds(pl.multiple_of(half * 256 + i * 64, 64), 64)
            wh[rows, cols] = high
            wl[rows, cols] = low
            return carry

        lax.fori_loop(0, NX, one, 0)

    def weights_done(s):
        for d in range(2):
            ring_z_done(d, s)
        weights_split(ring(z, 0, s))
        if 0 < s < 4:
            weights_split(ring(z, 1, s))

    def keys(h):
        cols = slice(h * HD, (h + 1) * HD)
        kf = features(k_ref[:, cols], km_ref[h])
        high, low = split(kf)
        kfh[h] = high
        kfl[h] = low
        st[h, 0:HD, :] = dot3(split(v_ref[:, cols].T), (high, low), NN)
        st[h, HD:SROWS, :] = jnp.broadcast_to(jnp.sum(kf, axis=0, keepdims=True), (SROWS - HD, FEAT))
        j = h % 4
        send(st.at[h], sp.at[j], dd_s.at[j], dd_r.at[j], (other, y), core != h // 4)

    def queries(h):
        cols = slice(h * HD, (h + 1) * HD)
        qf = split(features(q_ref[:, cols], qm_ref[h]))
        qfh[h], qfl[h] = qf
        w = dot3(qf, (kfh[h], kfl[h]), NT)
        causal = lax.broadcasted_iota(jnp.int32, (ROWS, ROWS), 0) >= lax.broadcasted_iota(jnp.int32, (ROWS, ROWS), 1)
        w = jnp.where(causal, w, 0.0)
        dl[h] = jnp.broadcast_to(jnp.sum(w, axis=1, keepdims=True), (ROWS, HD))
        nl[h] = dot3(split(w), split(v_ref[:, cols]), NN)

    def chip_sum(j):
        h = 4 * core + j
        recv(sp.at[j], dd_r.at[j])
        su[j] = st[h] + sp[j]
        send(su.at[j], rr.at[x], aa_s.at[j], aa_r.at[x], at(z, j), x != j)

        @pl.when(x == j)
        def _():
            rr[j] = su[j]

    def row_sum():
        for i in range(1, NX):
            xx = lax.rem(x + i, NX)
            recv(rr.at[xx], aa_r.at[xx])
        total = jnp.zeros((SROWS, FEAT), F32)
        for i in range(NX):
            bk[i] = total
            total = total + rr[i]
        for j in range(NZ):
            zt[j, 0:PIECE, :] = total[j * PIECE : (j + 1) * PIECE]
            zt[j, PIECE:, :] = total[HD:]
        for i in range(1, NZ):
            zz = lax.rem(z + i, NZ)
            send(zt.at[zz], zr.at[z], z1_s.at[i - 1], z1_r.at[z], at(zz, x))
        zr[z] = zt[z]

    def z_sum():
        for i in range(1, NZ):
            zz = lax.rem(z + i, NZ)
            recv(zr.at[zz], z1_r.at[zz])
        total = jnp.zeros((PIECE, FEAT), F32)
        norm = jnp.zeros((SROWS - HD, FEAT), F32)
        for j in range(NZ):
            zb[j] = total
            total = total + zr[j, 0:PIECE, :]
            norm = norm + jnp.where(j < z, zr[j, PIECE:, :], 0.0)
        rows = pl.ds(pl.multiple_of(z * PIECE, PIECE), PIECE)
        for i in range(1, NZ):
            zz = lax.rem(z + i, NZ)
            send(zb.at[zz], zp.at[rows, :], z2_s.at[i - 1], z2_r.at[z], at(zz, x))
        zp[rows, :] = zb[z]
        zp[HD:SROWS, :] = norm

    def send_back():
        for i in range(1, NZ):
            zz = lax.rem(z + i, NZ)
            recv(zp.at[pl.ds(pl.multiple_of(zz * PIECE, PIECE), PIECE), :], z2_r.at[zz])
        before = zp[...]
        for i in range(NX):
            bk[i] += before
            send(bk.at[i], pc.at[x], bb_s.at[i], bb_r.at[x], at(z, i), x != i)

            @pl.when(x == i)
            def _(i=i):
                pc[i] = bk[i]

    def cores_prefix():
        for j in range(4):
            if j == 0:
                for i in range(1, NX):
                    xx = lax.rem(x + i, NX)
                    recv(pc.at[xx], bb_r.at[xx])
            h = 4 * core + j
            low = pc[j]
            high = low + jnp.where(core == 0, st[h], sp[j])
            pf[h] = jnp.where(core == 0, low, high)
            sd[j] = jnp.where(core == 0, high, low)
            send(sd.at[j], pf.at[h], ee_s.at[j], ee_r.at[j], (other, y))

    def prefix_done():
        for j in range(4):
            recv(pf.at[4 * (1 - core) + j], ee_r.at[j])

    def mix(c):
        rows = pl.ds(c * CR, CR)
        for h in range(HEADS):
            state = pf[h]
            qf = (qfh[h, c * CR : (c + 1) * CR, :], qfl[h, c * CR : (c + 1) * CR, :])
            far_sum = dot3(qf, split(state), NT)
            denom = dl[h, c * CR : (c + 1) * CR, :] + far_sum[:, HD : HD + 1]
            ab[y, core, rows, h * HD : (h + 1) * HD] = (nl[h, c * CR : (c + 1) * CR, :] + far_sum[:, :HD]) / denom
        block = ab.at[y, core, rows, :]
        for k in range(2):
            send(block, block, m_s.at[c, k], m_r.at[c, k], (ctx, next_y(k)))
        send(block, block, m_s.at[c, 2], m_r.at[c, 4], (other, y))

    def next_y(k, n=1):
        return lax.rem(y + (n if k == 0 else NY - n), NY)

    def relay(c):
        for k in range(2):
            yy = next_y(1 - k)
            block = ab.at[yy, core, pl.ds(c * CR, CR), :]
            recv(block, m_r.at[c, k])
            half = ab.at[yy, core, pl.ds(c * CR + k * (CR // 2), CR // 2), :]
            send(half, half, m_s.at[c, 3 + k], m_r.at[c, 2 + k], (ctx, next_y(k)))
            send(block, block, m_s.at[c, 5 + k], m_r.at[c, 5 + k], (other, y))

    def relay_far(c):
        yy = next_y(0, 2)
        for k in range(2):
            recv(ab.at[yy, core, pl.ds(c * CR + k * (CR // 2), CR // 2), :], m_r.at[c, 2 + k])
        block = ab.at[yy, core, pl.ds(c * CR, CR), :]
        send(block, block, m_s.at[c, 7], m_r.at[c, 7], (other, y))

    def gather(c, places):
        for k in places:
            yy = (y, next_y(1), next_y(0), next_y(0, 2))[k]
            recv(ab.at[yy, 1 - core, pl.ds(c * CR, CR), :], m_r.at[c, 4 + k])
            for cc in range(2):
                high, low = split(ab[yy, cc, c * CR : (c + 1) * CR, :])
                rows, cols = slice(cc * ROWS + c * CR, cc * ROWS + (c + 1) * CR), pl.ds(pl.multiple_of(yy * WIDTH, WIDTH), WIDTH)
                ah[rows, cols] = high
                al[rows, cols] = low

    def project(n, m, places):
        owner = core if m == 0 else 1 - core
        rows = pl.ds(pl.multiple_of(owner * ROWS, ROWS), ROWS)
        wrows = slice(n * 256, (n + 1) * 256)
        total = None if 0 in places else co[n, m]
        for k in places:
            yy = (y, next_y(1), next_y(0), next_y(0, 2))[k]
            cols = pl.ds(pl.multiple_of(yy * WIDTH, WIDTH), WIDTH)
            term = dot3((ah[rows, cols], al[rows, cols]), (wh[wrows, cols], wl[wrows, cols]), NT)
            total = term if total is None else total + term
        co[n, m] = total
        if m and 3 in places:
            send(co.at[n, 1], fr.at[n], f_s.at[n], f_r.at[n], (other, y))

    def finish(n):
        recv(fr.at[n], f_r.at[n])
        low_half = lax.broadcasted_iota(jnp.int32, (ROWS, 128), 1) < 64
        for cc in range(2):

            @pl.when(core == cc)
            def _(cc=cc):
                for m in range(2):
                    cols = slice(m * 128, (m + 1) * 128)
                    a, b = co[n, 0, :, cols], fr[n, :, cols]
                    if cc:
                        a, b = b, a
                    start = n * 512 + m * 256
                    cols = slice(start, start + 128)
                    out_ref[:, cols] = res_ref[:, cols] + jnp.where(low_half, a, pltpu.roll(b, 64, 1))
                    cols = slice(start + 128, start + 256)
                    out_ref[:, cols] = res_ref[:, cols] + jnp.where(low_half, pltpu.roll(a, 64, 1), b)

    def ring_unit(s, i):
        for d in range(2):
            ring_x(d, s, i)
        if i == 0:
            for d in range(2):
                ring_z(d, s)
        if i == 2:
            for d in range(2):
                relay_z(d, s - 1)

    units = [(s, i) for s in range(1, 5) for i in range(NX)]

    def advance(n):
        for _ in range(n):
            if units:
                ring_unit(*units.pop(0))

    for n in (1, 2, 3):
        loads[n].wait()
    for j in range(4):
        keys(j)
        keys(4 + j)
        if j > 0:
            chip_sum(j - 1)
    chip_sum(3)
    weights_y_done()
    weights_x_send()
    for d in range(2):
        ring_x(d, 0, 0)
        ring_z(d, 0)
    for n in (4, 5):
        loads[n].wait()
    for h in range(0, 4):
        queries(h)
    row_sum()
    for h in range(4, 8):
        queries(h)
    z_sum()
    for i in range(1, NX):
        weights_x_done(i)
        for d in range(2):
            ring_x(d, 0, i)
    send_back()
    advance(2)
    cores_prefix()
    advance(1)
    prefix_done()
    near, across = (0, 1, 2), (3,)
    for c in range(CHUNKS):
        mix(c)
    advance(1)
    relay(0)
    advance(2)
    relay(1)
    advance(2)
    relay(2)
    advance(2)
    relay(3)
    advance(1)
    gather(0, near)
    advance(1)
    gather(1, near)
    relay_far(0)
    advance(2)
    for s in range(3):
        weights_done(s)
    gather(2, near)
    relay_far(1)
    advance(16)
    gather(3, near)
    for d in range(2):
        relay_z(d, 4)
    for s in (3, 4):
        weights_done(s)
    loads[6].wait()
    project(0, 1, near)
    relay_far(2)
    project(0, 0, near)
    relay_far(3)
    project(1, 1, near)
    project(1, 0, near)
    for c in range(CHUNKS):
        gather(c, across)
    for n in range(2):
        project(n, 1, across)
        project(n, 0, across)
        if n:
            finish(0)
    finish(1)
    for when, c in pending:
        if when is None:
            c.wait_send()
        else:
            pl.when(when)(c.wait_send)


def attend(q, k, v, qm, km, wt, res):
    dma = pltpu.SemaphoreType.DMA
    vmem = pltpu.VMEM
    block = vmem((ROWS, WIDTH), F32)
    maps = vmem((HEADS, HD, HD), F32)
    scratch = [
        block, block, block, maps, maps, vmem((16, NY * WIDTH), F32), block,
        vmem((HEADS, ROWS, FEAT), BF16), vmem((HEADS, ROWS, FEAT), BF16),
        vmem((HEADS, ROWS, FEAT), BF16), vmem((HEADS, ROWS, FEAT), BF16),
        vmem((HEADS, ROWS, HD), F32), vmem((HEADS, ROWS, HD), F32),
        vmem((HEADS, SROWS, FEAT), F32), vmem((4, SROWS, FEAT), F32), vmem((4, SROWS, FEAT), F32),
        vmem((NX, SROWS, FEAT), F32), vmem((NX, SROWS, FEAT), F32), vmem((NX, SROWS, FEAT), F32),
        vmem((4, SROWS, FEAT), F32), vmem((HEADS, SROWS, FEAT), F32),
        vmem((NZ, PIECE + 8, FEAT), F32), vmem((NZ, PIECE + 8, FEAT), F32),
        vmem((NZ, PIECE, FEAT), F32), vmem((SROWS, FEAT), F32),
        vmem((2, NX, 64, NY * WIDTH), F32), vmem((512, NY * WIDTH), BF16), vmem((512, NY * WIDTH), BF16),
        vmem((NY, 2, ROWS, WIDTH), F32), vmem((2 * ROWS, NY * WIDTH), BF16), vmem((2 * ROWS, NY * WIDTH), BF16),
        vmem((2, 2, ROWS, 256), F32), vmem((2, ROWS, 256), F32),
        dma((NY,)), dma((NY,)), dma((3,)), dma((NX,)),
        dma((2, 4, NX)), dma((2, 4, NX)), dma((2, 4)), dma((2, 4)),
        dma((2, 5, 4)), dma((2, 5, 4)),
        dma((4,)), dma((4,)), dma((4,)), dma((NX,)), dma((NZ - 1,)), dma((NZ,)), dma((NZ - 1,)), dma((NZ,)),
        dma((4,)), dma((NX,)), dma((4,)), dma((4,)),
        dma((CHUNKS, 8)), dma((CHUNKS, 8)), dma((2,)), dma((2,)),
        dma((7,)),
    ]
    return pl.pallas_call(
        kernel,
        out_shape=jax.ShapeDtypeStruct((ROWS, WIDTH), F32),
        in_specs=[pl.BlockSpec(memory_space=pl.ANY)] * 7,
        out_specs=pl.BlockSpec(memory_space=vmem),
        scratch_shapes=scratch,
        compiler_params=pltpu.CompilerParams(
            collective_id=0, has_side_effects=True, vmem_limit_bytes=60 * 1024 * 1024
        ),
    )(q, k, v, qm, km, wt, res)


def body(queries, keys, values, query_map, key_map, out_weight, residual):
    return attend(queries, keys, values, query_map, key_map, out_weight.T, residual)


def solution(mesh):
    placed = (
        P("ctx", "head"),
        P("ctx", "head"),
        P("ctx", "head"),
        P("head", None, None),
        P("head", None, None),
        P(None, ("ctx", "head")),
        P("ctx", "head"),
    )
    return jax.shard_map(body, mesh=mesh, in_specs=placed, out_specs=P("ctx", "head"), check_vma=False)
```

```python
import jax
import jax.numpy as jnp
from jax import lax
from jax.experimental import pallas as pl
from jax.experimental.pallas import tpu as pltpu
from jax.sharding import PartitionSpec as P

MESH = pl.DeviceIdType.MESH
NX, NY, NZ = 4, 4, 8
ROWS, HEADS, HD, FEAT = 256, 8, 128, 256
WIDTH = HEADS * HD
KP = 1024
KZ = 512
KX = KP - KZ
ZHALF = ((0, 256), (256, 256))
PIECE = 16
SROWS = 136
CHUNKS = 4
CR = ROWS // CHUNKS
F32, BF16 = jnp.float32, jnp.bfloat16

NN = (((1,), (0,)), ((), ()))
NT = (((1,), (1,)), ((), ()))


def split(a):
    high = a.astype(BF16)
    return high, (a - high.astype(F32)).astype(BF16)


def dot3(a, b, dims):
    (ah, al), (bh, bl) = a, b

    def one(p, q):
        return lax.dot_general(p, q, dims, preferred_element_type=F32)

    return one(ah, bh) + (one(ah, bl) + one(al, bh))


def features(inputs, weights):
    s = dot3(split(inputs), split(weights), NN)
    up = jnp.exp(s - jnp.max(s, axis=1, keepdims=True))
    down = jnp.exp(jnp.min(s, axis=1, keepdims=True) - s)
    up = up / jnp.sum(up, axis=1, keepdims=True)
    down = down / jnp.sum(down, axis=1, keepdims=True)
    return jnp.concatenate([up, down], axis=1)


def kernel(
    q_in, k_in, v_in, qm_in, km_in, wt_in, res_in, out_ref,
    q_ref, k_ref, v_ref, qm_ref, km_ref, wt_ref, res_ref,
    qfh, qfl, kfh, kfl, nl, dl, st, sp, su, rr, bk, pc, sd, pf, zt, zr, zb, zp,
    wb, wh, wl, ab, ah, al, co, fr,
    yg_s, yg_r, xa_s, xa_r, zx_s, zx_r, zz_s, zz_r, xz_s, xz_r,
    dd_s, dd_r, aa_s, aa_r, z1_s, z1_r, z2_s, z2_r, bb_s, bb_r, ee_s, ee_r, m_s, m_r, f_s, f_r, in_s,
):
    ctx, y = lax.axis_index("ctx"), lax.axis_index("head")
    core, r = lax.rem(ctx, 2), lax.rem(ctx, 8)
    x, z = lax.div(r, 2), lax.div(ctx, 8)
    other = ctx + 1 - 2 * core
    pending = []
    loads = {}
    inputs = (wt_in, wt_ref), (k_in, k_ref), (km_in, km_ref), (v_in, v_ref), (q_in, q_ref), (qm_in, qm_ref), (res_in, res_ref)
    for n, (src, dst) in enumerate(inputs):
        loads[n] = pltpu.make_async_copy(src, dst, in_s.at[n])
        loads[n].start()

    def at(zz, xx):
        return ((zz * NX + xx) * 2 + core, y)

    def copy(src, dst, send, recv, device):
        return pltpu.make_async_remote_copy(
            src_ref=src, dst_ref=dst, send_sem=send, recv_sem=recv, device_id=device, device_id_type=MESH
        )

    def send(src, dst, ss, rs, device, when=None):
        c = copy(src, dst, ss, rs, device)
        if when is None:
            c.start()
        else:
            pl.when(when)(c.start)
        pending.append((when, c))

    def recv(dst, rs, when=None):
        c = copy(dst, dst, rs, rs, (ctx, y))
        if when is None:
            c.wait_recv()
        else:
            pl.when(when)(c.wait_recv)

    barrier = pltpu.get_barrier_semaphore()
    greeted = [(ctx, lax.rem(y + i, NY)) for i in range(1, NY)]
    greeted += [at(z, lax.rem(x + i, NX)) for i in range(1, NX)] + [(other, y)]
    greeted += [at(lax.rem(z + i, NZ), x) for i in range(1, NZ)]
    for device in greeted:
        pl.semaphore_signal(barrier, inc=1, device_id=device, device_id_type=MESH)
    parity, zy = lax.rem(z, 2), lax.div(z, 2)
    for i in range(NY):
        to_there = at(2 * i + parity, x)[0]

        @pl.when(jnp.logical_or(i != zy, y != zy))
        def _(there=to_there):
            pl.semaphore_signal(barrier, inc=1, device_id=(there, zy), device_id_type=MESH)

        @pl.when(jnp.logical_or(i != y, y != zy))
        def _(i=i):
            pl.semaphore_signal(barrier, inc=1, device_id=(at(2 * y + parity, x)[0], i), device_id_type=MESH)

    pl.semaphore_wait(barrier, len(greeted) + jnp.where(y == zy, 6, 8))

    loads[0].wait()

    my_rows = pl.ds(pl.multiple_of(16 * y, 16), 16)
    for i in range(NY):
        cols = pl.ds(i * KP, KP)
        away = jnp.logical_or(i != zy, y != zy)
        dst = wb.at[parity, x, my_rows, cols]
        send(wt_ref.at[:, cols], dst, yg_s.at[i], yg_r.at[y], (at(2 * i + parity, x)[0], zy), away)

        @pl.when(jnp.logical_not(away))
        def _(i=i):
            wb[parity, x, my_rows, i * KP : (i + 1) * KP] = wt_ref[:, i * KP : (i + 1) * KP]

    def block_of(zz, xx, start, size):
        cols = pl.ds(pl.multiple_of(KP * lax.div(zz, 2) + start, 128), size)
        return wb.at[lax.rem(zz, 2), xx, :, cols]

    def weights_y_done():
        cols = pl.ds(pl.multiple_of(KP * zy, KP), KP)
        for i in range(NY):
            rows = pl.ds(16 * i, 16)
            recv(wb.at[parity, x, rows, cols], yg_r.at[i], jnp.logical_or(i != y, y != zy))

    def weights_x_send():
        for i in (1, 3, 2):
            xx = lax.rem(x + i, NX)
            block = block_of(z, x, KZ, KX)
            send(block, block, xa_s.at[i - 1], xa_r.at[x], at(z, xx))

    def weights_x_done(i):
        xx = lax.rem(x + i, NX)
        recv(block_of(z, xx, KZ, KX), xa_r.at[xx])

    def ring(zz, d, n):
        return lax.rem(zz + (n if d == 0 else NZ - n), NZ)

    def ring_x(d, s, i):
        xx = lax.rem(x + i, NX)
        block = block_of(ring(z, 1 - d, s), xx, KZ, KX)
        last = i // 2 == d
        if s > 0 and (s < 4 or last):
            recv(block, zx_r.at[d, s - 1, xx])
        if s < 3 or (s == 3 and last):
            send(block, block, zx_s.at[d, s, xx], zx_r.at[d, s, xx], at(ring(z, d, 1), x))

    def ring_z(d, s):
        source = ring(z, 1 - d, s)
        start, size = ZHALF[d] if s == 4 else (0, KZ)
        block = block_of(source, x, start, size)
        if s > 0:
            recv(block, zz_r.at[d, s - 1])
        if s < 4:
            start, size = ZHALF[d] if s == 3 else (0, KZ)
            part = block_of(source, x, start, size)
            send(part, part, zz_s.at[d, s], zz_r.at[d, s], at(ring(z, d, 1), x))
        if s > 0 or d == 0:
            for k in range(2):
                send(block, block, xz_s.at[d, s, k], xz_r.at[d, s, k], at(z, beside(k)))

    def beside(k, n=1):
        return lax.rem(x + (n if k == 0 else NX - n), NX)

    def part_of(start, size, k):
        cut = size // 256 * 128
        return (start, cut) if k == 0 else (start + cut, size - cut)

    def relay_z(d, s):
        if s == 0 and d == 1:
            return
        source = ring(z, 1 - d, s)
        start, size = ZHALF[d] if s == 4 else (0, KZ)
        for k in range(2):
            recv(block_of(source, beside(1 - k), start, size), xz_r.at[d, s, k])
            half = block_of(source, beside(1 - k), *part_of(start, size, k))
            send(half, half, xz_s.at[d, s, 2 + k], xz_r.at[d, s, 2 + k], at(z, beside(k)))

    def ring_z_done(d, s):
        if s == 0 and d == 1:
            return
        source = ring(z, 1 - d, s)
        start, size = ZHALF[d] if s == 4 else (0, KZ)
        for k in range(2):
            recv(block_of(source, beside(1 - k, 2), *part_of(start, size, k)), xz_r.at[d, s, 2 + k])

    def weights_split(zz):
        cols = pl.ds(pl.multiple_of(KP * lax.div(zz, 2), KP), KP)
        half = lax.rem(zz, 2)

        def one(i, carry):
            high, low = split(wb[half, i, :, cols])
            rows = pl.ds(pl.multiple_of(half * 256 + i * 64, 64), 64)
            wh[rows, cols] = high
            wl[rows, cols] = low
            return carry

        lax.fori_loop(0, NX, one, 0)

    def weights_done(s):
        for d in range(2):
            ring_z_done(d, s)
        weights_split(ring(z, 0, s))
        if 0 < s < 4:
            weights_split(ring(z, 1, s))

    def keys(h):
        cols = slice(h * HD, (h + 1) * HD)
        kf = features(k_ref[:, cols], km_ref[h])
        high, low = split(kf)
        kfh[h] = high
        kfl[h] = low
        st[h, 0:HD, :] = dot3(split(v_ref[:, cols].T), (high, low), NN)
        st[h, HD:SROWS, :] = jnp.broadcast_to(jnp.sum(kf, axis=0, keepdims=True), (SROWS - HD, FEAT))
        j = h % 4
        send(st.at[h], sp.at[j], dd_s.at[j], dd_r.at[j], (other, y), core != h // 4)

    def queries(h):
        cols = slice(h * HD, (h + 1) * HD)
        qf = split(features(q_ref[:, cols], qm_ref[h]))
        qfh[h], qfl[h] = qf
        w = dot3(qf, (kfh[h], kfl[h]), NT)
        causal = lax.broadcasted_iota(jnp.int32, (ROWS, ROWS), 0) >= lax.broadcasted_iota(jnp.int32, (ROWS, ROWS), 1)
        w = jnp.where(causal, w, 0.0)
        dl[h] = jnp.broadcast_to(jnp.sum(w, axis=1, keepdims=True), (ROWS, HD))
        nl[h] = dot3(split(w), split(v_ref[:, cols]), NN)

    def chip_sum(j):
        h = 4 * core + j
        recv(sp.at[j], dd_r.at[j])
        su[j] = st[h] + sp[j]
        send(su.at[j], rr.at[x], aa_s.at[j], aa_r.at[x], at(z, j), x != j)

        @pl.when(x == j)
        def _():
            rr[j] = su[j]

    def row_sum():
        for i in range(1, NX):
            xx = lax.rem(x + i, NX)
            recv(rr.at[xx], aa_r.at[xx])
        total = jnp.zeros((SROWS, FEAT), F32)
        for i in range(NX):
            bk[i] = total
            total = total + rr[i]
        for j in range(NZ):
            zt[j, 0:PIECE, :] = total[j * PIECE : (j + 1) * PIECE]
            zt[j, PIECE:, :] = total[HD:]
        for i in range(1, NZ):
            zz = lax.rem(z + i, NZ)
            send(zt.at[zz], zr.at[z], z1_s.at[i - 1], z1_r.at[z], at(zz, x))
        zr[z] = zt[z]

    def z_sum():
        for i in range(1, NZ):
            zz = lax.rem(z + i, NZ)
            recv(zr.at[zz], z1_r.at[zz])
        total = jnp.zeros((PIECE, FEAT), F32)
        norm = jnp.zeros((SROWS - HD, FEAT), F32)
        for j in range(NZ):
            zb[j] = total
            total = total + zr[j, 0:PIECE, :]
            norm = norm + jnp.where(j < z, zr[j, PIECE:, :], 0.0)
        rows = pl.ds(pl.multiple_of(z * PIECE, PIECE), PIECE)
        for i in range(1, NZ):
            zz = lax.rem(z + i, NZ)
            send(zb.at[zz], zp.at[rows, :], z2_s.at[i - 1], z2_r.at[z], at(zz, x))
        zp[rows, :] = zb[z]
        zp[HD:SROWS, :] = norm

    def send_back():
        for i in range(1, NZ):
            zz = lax.rem(z + i, NZ)
            recv(zp.at[pl.ds(pl.multiple_of(zz * PIECE, PIECE), PIECE), :], z2_r.at[zz])
        before = zp[...]
        for i in range(NX):
            bk[i] += before
            send(bk.at[i], pc.at[x], bb_s.at[i], bb_r.at[x], at(z, i), x != i)

            @pl.when(x == i)
            def _(i=i):
                pc[i] = bk[i]

    def cores_prefix():
        for j in range(4):
            if j == 0:
                for i in range(1, NX):
                    xx = lax.rem(x + i, NX)
                    recv(pc.at[xx], bb_r.at[xx])
            h = 4 * core + j
            low = pc[j]
            high = low + jnp.where(core == 0, st[h], sp[j])
            pf[h] = jnp.where(core == 0, low, high)
            sd[j] = jnp.where(core == 0, high, low)
            send(sd.at[j], pf.at[h], ee_s.at[j], ee_r.at[j], (other, y))

    def prefix_done():
        for j in range(4):
            recv(pf.at[4 * (1 - core) + j], ee_r.at[j])

    def mix(c):
        rows = pl.ds(c * CR, CR)
        for h in range(HEADS):
            state = pf[h]
            qf = (qfh[h, c * CR : (c + 1) * CR, :], qfl[h, c * CR : (c + 1) * CR, :])
            far_sum = dot3(qf, split(state), NT)
            denom = dl[h, c * CR : (c + 1) * CR, :] + far_sum[:, HD : HD + 1]
            ab[y, core, rows, h * HD : (h + 1) * HD] = (nl[h, c * CR : (c + 1) * CR, :] + far_sum[:, :HD]) / denom
        block = ab.at[y, core, rows, :]
        for k in range(2):
            send(block, block, m_s.at[c, k], m_r.at[c, k], (ctx, next_y(k)))
        send(block, block, m_s.at[c, 2], m_r.at[c, 4], (other, y))

    def next_y(k, n=1):
        return lax.rem(y + (n if k == 0 else NY - n), NY)

    def relay(c):
        for k in range(2):
            yy = next_y(1 - k)
            block = ab.at[yy, core, pl.ds(c * CR, CR), :]
            recv(block, m_r.at[c, k])
            half = ab.at[yy, core, pl.ds(c * CR + k * (CR // 2), CR // 2), :]
            send(half, half, m_s.at[c, 3 + k], m_r.at[c, 2 + k], (ctx, next_y(k)))
            send(block, block, m_s.at[c, 5 + k], m_r.at[c, 5 + k], (other, y))

    def relay_far(c):
        yy = next_y(0, 2)
        for k in range(2):
            recv(ab.at[yy, core, pl.ds(c * CR + k * (CR // 2), CR // 2), :], m_r.at[c, 2 + k])
        block = ab.at[yy, core, pl.ds(c * CR, CR), :]
        send(block, block, m_s.at[c, 7], m_r.at[c, 7], (other, y))

    def gather(c, places):
        for k in places:
            yy = (y, next_y(1), next_y(0), next_y(0, 2))[k]
            recv(ab.at[yy, 1 - core, pl.ds(c * CR, CR), :], m_r.at[c, 4 + k])
            for cc in range(2):
                high, low = split(ab[yy, cc, c * CR : (c + 1) * CR, :])
                rows, cols = slice(cc * ROWS + c * CR, cc * ROWS + (c + 1) * CR), pl.ds(pl.multiple_of(yy * WIDTH, WIDTH), WIDTH)
                ah[rows, cols] = high
                al[rows, cols] = low

    def project(n, m, places):
        owner = core if m == 0 else 1 - core
        rows = pl.ds(pl.multiple_of(owner * ROWS, ROWS), ROWS)
        wrows = slice(n * 256, (n + 1) * 256)
        total = None if 0 in places else co[n, m]
        for k in places:
            yy = (y, next_y(1), next_y(0), next_y(0, 2))[k]
            cols = pl.ds(pl.multiple_of(yy * WIDTH, WIDTH), WIDTH)
            term = dot3((ah[rows, cols], al[rows, cols]), (wh[wrows, cols], wl[wrows, cols]), NT)
            total = term if total is None else total + term
        co[n, m] = total
        if m and 3 in places:
            send(co.at[n, 1], fr.at[n], f_s.at[n], f_r.at[n], (other, y))

    def finish(n):
        recv(fr.at[n], f_r.at[n])
        low_half = lax.broadcasted_iota(jnp.int32, (ROWS, 128), 1) < 64
        for cc in range(2):

            @pl.when(core == cc)
            def _(cc=cc):
                for m in range(2):
                    cols = slice(m * 128, (m + 1) * 128)
                    a, b = co[n, 0, :, cols], fr[n, :, cols]
                    if cc:
                        a, b = b, a
                    start = n * 512 + m * 256
                    cols = slice(start, start + 128)
                    out_ref[:, cols] = res_ref[:, cols] + jnp.where(low_half, a, pltpu.roll(b, 64, 1))
                    cols = slice(start + 128, start + 256)
                    out_ref[:, cols] = res_ref[:, cols] + jnp.where(low_half, pltpu.roll(a, 64, 1), b)

    def ring_unit(s, i):
        for d in range(2):
            ring_x(d, s, i)
        if i == 0:
            for d in range(2):
                ring_z(d, s)
        if i == 3:
            for d in range(2):
                relay_z(d, s - 1)

    units = [(s, i) for s in range(1, 5) for i in (0, 1, 3, 2)]

    def advance(n):
        for _ in range(n):
            if units:
                ring_unit(*units.pop(0))

    for n in (1, 2, 3):
        loads[n].wait()
    for j in range(4):
        keys(j)
        keys(4 + j)
        if j > 0:
            chip_sum(j - 1)
    chip_sum(3)
    weights_y_done()
    weights_x_send()
    for d in range(2):
        ring_x(d, 0, 0)
        ring_z(d, 0)
    for n in (4, 5):
        loads[n].wait()
    for h in range(0, 4):
        queries(h)
    row_sum()
    for h in range(4, 8):
        queries(h)
    weights_x_done(1)
    for d in range(2):
        ring_x(d, 0, 1)
    z_sum()
    for i in (3, 2):
        weights_x_done(i)
        for d in range(2):
            ring_x(d, 0, i)
    send_back()
    advance(3)
    cores_prefix()
    advance(1)
    prefix_done()
    near, across = (0, 1, 2), (3,)
    for c in range(CHUNKS):
        mix(c)
    advance(1)
    relay(0)
    advance(2)
    relay(1)
    advance(2)
    relay(2)
    advance(2)
    relay(3)
    advance(1)
    gather(0, near)
    advance(1)
    gather(1, near)
    relay_far(0)
    advance(2)
    for s in range(3):
        weights_done(s)
    gather(2, near)
    relay_far(1)
    advance(16)
    gather(3, near)
    for d in range(2):
        relay_z(d, 4)
    for s in (3, 4):
        weights_done(s)
    loads[6].wait()
    project(0, 1, near)
    relay_far(2)
    project(0, 0, near)
    relay_far(3)
    project(1, 1, near)
    project(1, 0, near)
    for c in range(CHUNKS):
        gather(c, across)
    for n in range(2):
        project(n, 1, across)
        project(n, 0, across)
        if n:
            finish(0)
    finish(1)
    for when, c in pending:
        if when is None:
            c.wait_send()
        else:
            pl.when(when)(c.wait_send)


def attend(q, k, v, qm, km, wt, res):
    dma = pltpu.SemaphoreType.DMA
    vmem = pltpu.VMEM
    block = vmem((ROWS, WIDTH), F32)
    maps = vmem((HEADS, HD, HD), F32)
    scratch = [
        block, block, block, maps, maps, vmem((16, NY * WIDTH), F32), block,
        vmem((HEADS, ROWS, FEAT), BF16), vmem((HEADS, ROWS, FEAT), BF16),
        vmem((HEADS, ROWS, FEAT), BF16), vmem((HEADS, ROWS, FEAT), BF16),
        vmem((HEADS, ROWS, HD), F32), vmem((HEADS, ROWS, HD), F32),
        vmem((HEADS, SROWS, FEAT), F32), vmem((4, SROWS, FEAT), F32), vmem((4, SROWS, FEAT), F32),
        vmem((NX, SROWS, FEAT), F32), vmem((NX, SROWS, FEAT), F32), vmem((NX, SROWS, FEAT), F32),
        vmem((4, SROWS, FEAT), F32), vmem((HEADS, SROWS, FEAT), F32),
        vmem((NZ, PIECE + 8, FEAT), F32), vmem((NZ, PIECE + 8, FEAT), F32),
        vmem((NZ, PIECE, FEAT), F32), vmem((SROWS, FEAT), F32),
        vmem((2, NX, 64, NY * WIDTH), F32), vmem((512, NY * WIDTH), BF16), vmem((512, NY * WIDTH), BF16),
        vmem((NY, 2, ROWS, WIDTH), F32), vmem((2 * ROWS, NY * WIDTH), BF16), vmem((2 * ROWS, NY * WIDTH), BF16),
        vmem((2, 2, ROWS, 256), F32), vmem((2, ROWS, 256), F32),
        dma((NY,)), dma((NY,)), dma((3,)), dma((NX,)),
        dma((2, 4, NX)), dma((2, 4, NX)), dma((2, 4)), dma((2, 4)),
        dma((2, 5, 4)), dma((2, 5, 4)),
        dma((4,)), dma((4,)), dma((4,)), dma((NX,)), dma((NZ - 1,)), dma((NZ,)), dma((NZ - 1,)), dma((NZ,)),
        dma((4,)), dma((NX,)), dma((4,)), dma((4,)),
        dma((CHUNKS, 8)), dma((CHUNKS, 8)), dma((2,)), dma((2,)),
        dma((7,)),
    ]
    return pl.pallas_call(
        kernel,
        out_shape=jax.ShapeDtypeStruct((ROWS, WIDTH), F32),
        in_specs=[pl.BlockSpec(memory_space=pl.ANY)] * 7,
        out_specs=pl.BlockSpec(memory_space=vmem),
        scratch_shapes=scratch,
        compiler_params=pltpu.CompilerParams(
            collective_id=0, has_side_effects=True, vmem_limit_bytes=60 * 1024 * 1024
        ),
    )(q, k, v, qm, km, wt, res)


def body(queries, keys, values, query_map, key_map, out_weight, residual):
    return attend(queries, keys, values, query_map, key_map, out_weight.T, residual)


def solution(mesh):
    placed = (
        P("ctx", "head"),
        P("ctx", "head"),
        P("ctx", "head"),
        P("head", None, None),
        P("head", None, None),
        P(None, ("ctx", "head")),
        P("ctx", "head"),
    )
    return jax.shard_map(body, mesh=mesh, in_specs=placed, out_specs=P("ctx", "head"), check_vma=False)
```
